128 devices in a mesh: layer: 16 (over z, x_lo, core), feat: 8 (over x_hi, y).
Axes of the slice: x: 4 (x_hi: 2, x_lo: 2; x = x_hi * 2 + x_lo), y: 4, z: 4, core: 2. Of those that a mesh axis runs over, the one named last changes fastest.
Arguments:
- attn_heads: bfloat16 [16, 768, 2048], P('layer', None, 'feat'), may hold values from -6 to 6
- out_proj: bfloat16 [16, 2048, 2048], P('layer', 'feat'), may hold values from -0.125 to 0.125
- resid_pre: bfloat16 [16, 768, 2048], P('layer'), may hold values from -6 to 6
- enc_weight: bfloat16 [16, 2048, 16384], P('layer', None, 'feat'), may hold values from -0.0234375 to 0.0234375
- enc_bias: float32 [16384], P('feat'), may hold values from -4 to 4
- dec_weight: bfloat16 [16, 16384, 2048], P('layer', 'feat'), may hold values from -0.09375 to 0.09375
- dec_bias: float32 [16, 2048], P('layer', 'feat'), may hold values from -3 to 3
Outputs:
- features: float32 [768, 16384], P('layer', 'feat')
- rebuilt: float32 [16, 768, 2048], P('layer', None, 'feat')
The draws below stay inside these ranges and needn't reach their ends.
All inputs are finite; a program needn't handle non-finite values.
Results may differ from the reference program's by a relative error of at most 0.0035.
Values may be sent and summed in bfloat16 or wider, within the bound.
A program may use at most 128 MiB of HBM per device.

```python
import jax
import jax.numpy as jnp

D = 2048
FEATS = 16384
TOKENS = 768
LAYERS = 16


def levels(rng, extent, pieces, low, largest):
    level, own = 1.0, jax.random.fold_in(rng, 6)
    for axis_at, parts in pieces:
        heights = jnp.exp(jax.random.uniform(jax.random.fold_in(own, axis_at), (parts,), jnp.float32, low / len(pieces), largest / len(pieces)))
        level = level * jnp.repeat(heights, extent[axis_at] // parts).reshape([-1 if axis == axis_at else 1 for axis in range(len(extent))])
    return level


def normal_values(own_key, extent, spread, bound, pieces=(), held_as=jnp.bfloat16):
    array = spread * jax.random.normal(own_key, extent, jnp.float32)
    if pieces:
        array = array * levels(own_key, extent, pieces, -0.22, 0.18)
    return jnp.clip(array, -bound, bound).astype(held_as)


def setup_inputs(seed: int = 0) -> dict:
    streams_of = jax.random.split(jax.random.key(seed), 8)
    return {
        "attn_heads": normal_values(streams_of[0], (LAYERS, TOKENS, D), 1.0, 6.0, ((0, 16), (2, 8))),
        "out_proj": normal_values(streams_of[1], (LAYERS, D, D), D ** -0.5, 0.125, ((0, 16), (1, 8))),
        "resid_pre": normal_values(streams_of[2], (LAYERS, TOKENS, D), 1.0, 6.0, ((0, 16),)),
        "enc_weight": normal_values(streams_of[3], (LAYERS, D, FEATS), (2 * D * LAYERS) ** -0.5, 0.0234375, ((0, 16), (2, 8))),
        "enc_bias": normal_values(streams_of[4], (FEATS,), 0.7, 4.0, ((0, 8),), jnp.float32),
        "dec_weight": normal_values(streams_of[5], (LAYERS, FEATS, D), (FEATS // 4) ** -0.5, 0.09375, ((0, 16), (1, 8))),
        "dec_bias": normal_values(streams_of[6], (LAYERS, D), 0.5, 3.0, ((0, 16), (1, 8)), jnp.float32),
    }


def reference(attn_heads, out_proj, resid_pre, enc_weight, enc_bias, dec_weight, dec_bias):
    preact = jnp.zeros((TOKENS, FEATS), jnp.float32) + enc_bias[None, :]
    for layer in range(LAYERS):
        projected = jnp.dot(attn_heads[layer], out_proj[layer], preferred_element_type=jnp.float32)
        hidden_in = (resid_pre[layer].astype(jnp.float32) + projected).astype(jnp.bfloat16)
        preact = preact + jnp.dot(hidden_in, enc_weight[layer], preferred_element_type=jnp.float32)
    features = jnp.maximum(preact, 0.0)
    coded = features.astype(jnp.bfloat16)
    outputs = []
    for layer in range(LAYERS):
        outputs.append(dec_bias[layer][None, :] + jnp.dot(coded, dec_weight[layer], preferred_element_type=jnp.float32))
    return features, jnp.stack(outputs, axis=0)
```

```python
import functools
import itertools

import jax
import jax.numpy as jnp
from jax import lax
from jax.experimental import pallas as pl
from jax.experimental.pallas import tpu as pltpu
from jax.sharding import PartitionSpec as P

MESH = pl.DeviceIdType.MESH
LAYERS, FEATS = 16, 8
ROWS = 16
SEMS = 160
F32, BF16 = jnp.float32, jnp.bfloat16

STEPS = (
    ("relay_heads", 6, 5),
    ("project", 12, 7),
    ("hide", 19, 9),
    ("spread_own", 23, 9),
    ("spread_partner", 25, 9),
    ("relay_partner", 30, 9),
    ("encode", 36, 9),
    ("sum_core", 41, 9),
    ("sum_far", 44, 9),
    ("sum_near", 48, 9),
    ("activate", 51, 9),
    ("gather_pair", 53, 9),
    ("gather_far", 56, 9),
    ("gather_core", 59, 9),
    ("decode", 61, 9),
    ("sum_relay", 67, 9),
    ("sum_ring", 71, 9),
    ("finish", 76, 9),
)


def dot(a, b):
    return jnp.dot(a, b, preferred_element_type=F32)


def at(start, size):
    return pl.ds(pl.multiple_of(start, size), size)


def kernel(
    chunks, heads, out_proj, resid, enc, enc_bias, dec, dec_bias, features, rebuilt,
    hbuf, obuf, rbuf, psend, precv, pown, hid, encv, decv, ebuf, erecv, zfar, znear, ztot, xlrecv, coded,
    far_up, far_down, own, s1, r1, s2, r2, s3, r3, send_sem, recv_sem, local_sem,
):
    layer, feat = lax.axis_index("layer"), lax.axis_index("feat")
    z, xl, core = layer // 4, lax.rem(layer // 2, 2), lax.rem(layer, 2)
    xh, y = feat // 4, lax.rem(feat, 4)
    yc = [lax.rem(y + k, 4) for k in range(4)]
    zc = [lax.rem(z + k, 4) for k in range(4)]
    y_at = [{"feat": xh * 4 + yc[k]} for k in range(4)]
    z_at = [{"layer": zc[k] * 4 + xl * 2 + core} for k in range(4)]
    x_at = {"feat": (1 - xh) * 4 + y}
    xl_at = {"layer": z * 4 + (1 - xl) * 2 + core}
    core_at = {"layer": z * 4 + xl * 2 + 1 - core}
    slot = out_proj.shape[0]
    half = 4 * slot
    token_rows = LAYERS * ROWS
    side = token_rows // 2
    feats = encv.shape[1]

    locals_, remotes = itertools.count(), itertools.count()
    sent = []

    def local(src, dst):
        copy = pltpu.make_async_copy(src, dst, local_sem.at[next(locals_)])
        copy.start()
        return copy

    def send(src, dst, where):
        index = next(remotes)
        copy = pltpu.make_async_remote_copy(
            src, dst, send_sem.at[index], recv_sem.at[index], device_id=where, device_id_type=MESH
        )
        copy.start()
        sent.append(copy)
        return copy

    def rows(t):
        return pl.ds(t * ROWS, ROWS)

    def group(which_z, which_xl):
        return at((core * 8 + which_z * 2 + which_xl) * ROWS, ROWS)

    def block(which_z):
        return at((core * 8 + which_z * 2) * ROWS, 2 * ROWS)

    own_cols = at(feat * slot, slot)
    partner_cols = at(((1 - xh) * 4 + y) * slot, slot)

    fetched = {}
    for t in range(chunks):
        for c in range(2):
            fetched["heads", t, c] = local(heads.at[:, c, rows(t), :], hbuf.at[t, c, :, :, at(y * slot, slot)])
    for j in range(2):
        fetched["proj", j] = local(
            out_proj.at[:, at(j * half + y * slot, slot)], obuf.at[at(y * slot, slot), pl.ds(j * slot, slot)]
        )
    for t in range(chunks):
        for c in range(2):
            fetched["resid", t, c] = local(resid.at[:, c, rows(t), own_cols], rbuf.at[t, c])
    fetched["enc"] = local(enc, encv)
    fetched["dec"] = local(dec, decv)

    barrier = pltpu.get_barrier_semaphore()
    greeted = [y_at[1], y_at[2], y_at[3], z_at[1], z_at[3], x_at, xl_at, core_at]
    for where in greeted:
        pl.semaphore_signal(barrier, inc=1, device_id=where, device_id_type=MESH)
    pl.semaphore_wait(barrier, len(greeted))

    came = {}

    def send_heads(t):
        for c, k in ((0, 1), (1, 3), (1, 1), (0, 3)):
            came["heads", t, c, k] = send(
                heads.at[:, c, rows(t), :], hbuf.at[t, c, :, :, at(y * slot, slot)], y_at[k]
            )

    send_heads(0)
    for k in (1, 3, 2):
        for j in range(2):
            came["proj", k, j] = send(
                out_proj.at[:, at(j * half + yc[k] * slot, slot)],
                obuf.at[at(y * slot, slot), pl.ds(j * slot, slot)],
                y_at[k],
            )
    for t in range(1, chunks):
        send_heads(t)

    def relay_heads(t):
        for c, k, back in ((0, 1, 3), (1, 3, 1)):
            came["heads", t, c, k].wait_recv()
            part = hbuf.at[t, c, :, :, at(yc[back] * slot, slot)]
            came["heads2", t, c] = send(part, part, y_at[k])

    def project(t):
        if t == 0:
            for j in range(2):
                fetched["proj", j].wait()
            for k in (1, 3, 2):
                for j in range(2):
                    came["proj", k, j].wait_recv()
        for c in range(2):
            fetched["heads", t, c].wait()
            fetched["resid", t, c].wait()
        for c, k in ((1, 1), (0, 3)):
            came["heads", t, c, k].wait_recv()
        for c in range(2):
            came["heads2", t, c].wait_recv()
        lhs = hbuf[t].reshape(token_rows, half)
        psend[t] = dot(lhs, obuf[:, at((1 - xh) * slot, slot)])
        came["part", t] = send(psend.at[t], precv.at[t], x_at)
        pown[t] = dot(lhs, obuf[:, at(xh * slot, slot)])

    def ring_send(name, t, cols):
        for h, k in ((0, 1), (1, 3), (1, 1), (0, 3)):
            part = hid.at[t, pl.ds(h * side, side), cols]
            came[name, t, h, k] = send(part, part, y_at[k])

    def ring_relay(name, t, which_xh):
        for h, k, back in ((0, 1, 3), (1, 3, 1)):
            came[name, t, h, k].wait_recv()
            part = hid.at[t, pl.ds(h * side, side), at((which_xh * 4 + yc[back]) * slot, slot)]
            came[name + "2", t, h] = send(part, part, y_at[k])

    def ring_wait(name, t):
        for h, k in ((1, 1), (0, 3)):
            came[name, t, h, k].wait_recv()
        for h in range(2):
            came[name + "2", t, h].wait_recv()

    def hide(t):
        came["part", t].wait_recv()
        projected = pown[t] + precv[t]
        residual = rbuf[t].reshape(token_rows, slot).astype(F32)
        hid[t, :, own_cols] = (residual + projected).astype(BF16)
        part = hid.at[t, :, own_cols]
        came["pair", t] = send(part, part, x_at)
        ring_send("ring", t, own_cols)

    def spread_own(t):
        ring_relay("ring", t, xh)

    def spread_partner(t):
        came["pair", t].wait_recv()
        ring_send("other", t, partner_cols)

    def relay_partner(t):
        ring_relay("other", t, 1 - xh)

    def encode(t):
        if t == 0:
            fetched["enc"].wait()
        ring_wait("ring", t)
        ring_wait("other", t)
        width = feats // 2
        for piece in range(2):

            def tile(n, carry):
                cols = at(piece * width + n * 256, 256)
                ebuf[t, :, cols] = dot(hid[t], encv[:, cols])
                return carry

            lax.fori_loop(0, width // 256, tile, 0)
            cols = pl.ds(piece * width, width)
            came["core", t, piece] = send(
                ebuf.at[t, at((1 - core) * side, side), cols], erecv.at[t, :, cols], core_at
            )

    def sum_core(t):
        width = feats // 2
        mine = at(core * side, side)
        for piece in range(2):
            cols = pl.ds(piece * width, width)
            came["core", t, piece].wait_recv()
            ebuf[t, mine, cols] = ebuf[t, mine, cols] + erecv[t, :, cols]
        came["zfar", t, 0] = send(ebuf.at[t, group(zc[2], xl)], zfar.at[t, 0], z_at[1])
        came["zfar", t, 1] = send(ebuf.at[t, group(zc[2], 1 - xl)], zfar.at[t, 1], z_at[3])
        came["znear", t, 0, 1] = send(ebuf.at[t, group(zc[1], 1 - xl)], znear.at[t, 0, 1], z_at[1])
        came["znear", t, 1, 0] = send(ebuf.at[t, group(zc[3], xl)], znear.at[t, 1, 0], z_at[3])

    def sum_far(t):
        came["zfar", t, 0].wait_recv()
        here = group(zc[1], xl)
        ebuf[t, here] = ebuf[t, here] + zfar[t, 0]
        came["znear", t, 0, 0] = send(ebuf.at[t, here], znear.at[t, 0, 0], z_at[1])
        came["zfar", t, 1].wait_recv()
        here = group(zc[3], 1 - xl)
        ebuf[t, here] = ebuf[t, here] + zfar[t, 1]
        came["znear", t, 1, 1] = send(ebuf.at[t, here], znear.at[t, 1, 1], z_at[3])

    def sum_near(t):
        for kind, which in ((1, 1 - xl), (0, xl)):
            came["znear", t, 0, kind].wait_recv()
            came["znear", t, 1, kind].wait_recv()
            ztot[t, kind] = ebuf[t, group(z, which)] + znear[t, 0, kind] + znear[t, 1, kind]
            if kind == 1:
                came["xl", t] = send(ztot.at[t, 1], xlrecv.at[t], xl_at)

    def activate(t):
        came["xl", t].wait_recv()
        active = jnp.maximum(ztot[t, 0] + xlrecv[t] + enc_bias[...], 0.0)
        features[pl.ds(t * ROWS, ROWS), :] = active
        here = group(z, xl)
        coded[t, here] = active.astype(BF16)
        part = coded.at[t, here]
        came["cpair", t] = send(part, part, xl_at)
        came["cown", t, 1] = send(part, part, z_at[1])
        came["cown", t, 3] = send(part, part, z_at[3])

    def gather_pair(t):
        came["cpair", t].wait_recv()
        part = coded.at[t, group(z, 1 - xl)]
        came["cother", t, 1] = send(part, part, z_at[1])
        came["cother", t, 3] = send(part, part, z_at[3])
        part = coded.at[t, block(z)]
        came["ccore", t, 0] = send(part, part, core_at)

    def gather_far(t):
        came["cown", t, 1].wait_recv()
        part = coded.at[t, group(zc[3], xl)]
        came["cown2", t] = send(part, part, z_at[1])
        came["cother", t, 3].wait_recv()
        part = coded.at[t, group(zc[1], 1 - xl)]
        came["cother2", t] = send(part, part, z_at[3])
        came["cother", t, 1].wait_recv()
        part = coded.at[t, block(zc[3])]
        came["ccore", t, 3] = send(part, part, core_at)
        came["cown", t, 3].wait_recv()
        part = coded.at[t, block(zc[1])]
        came["ccore", t, 1] = send(part, part, core_at)

    def gather_core(t):
        came["cown2", t].wait_recv()
        came["cother2", t].wait_recv()
        part = coded.at[t, block(zc[2])]
        came["ccore", t, 2] = send(part, part, core_at)

    def decode(t):
        if t == 0:
            fetched["dec"].wait()
        for k in range(4):
            came["ccore", t, k].wait_recv()

        def to(which, store):
            def tile(j, carry):
                out = dot(coded[t], decv[:, at(j * half + yc[which] * slot, slot)])
                store(at(j * slot, slot), out[:side], out[side:])
                return carry

            lax.fori_loop(0, 2, tile, 0)

        def store_far(cols, low, high):
            s1[t, 0, :, cols] = low.astype(BF16)
            s1[t, 1, :, cols] = high.astype(BF16)

        def store_up(cols, low, high):
            far_up[t, :, cols] = low
            s2[t, 0, 1, :, cols] = high.astype(BF16)

        def store_down(cols, low, high):
            s2[t, 1, 0, :, cols] = low.astype(BF16)
            far_down[t, :, cols] = high

        def store_own(cols, low, high):
            own[t, 0, :, cols] = low
            own[t, 1, :, cols] = high

        to(2, store_far)
        came["r1", t, 0] = send(s1.at[t, 0], r1.at[t, 0], y_at[1])
        came["r1", t, 1] = send(s1.at[t, 1], r1.at[t, 1], y_at[3])
        to(1, store_up)
        came["r2", t, 0, 1] = send(s2.at[t, 0, 1], r2.at[t, 0, 1], y_at[1])
        to(3, store_down)
        came["r2", t, 1, 0] = send(s2.at[t, 1, 0], r2.at[t, 1, 0], y_at[3])
        to(0, store_own)

    def sum_relay(t):
        came["r1", t, 0].wait_recv()
        s2[t, 0, 0] = (far_up[t] + r1[t, 0].astype(F32)).astype(BF16)
        came["r2", t, 0, 0] = send(s2.at[t, 0, 0], r2.at[t, 0, 0], y_at[1])
        came["r1", t, 1].wait_recv()
        s2[t, 1, 1] = (far_down[t] + r1[t, 1].astype(F32)).astype(BF16)
        came["r2", t, 1, 1] = send(s2.at[t, 1, 1], r2.at[t, 1, 1], y_at[3])

    def sum_ring(t):
        for d in range(2):
            for h in range(2):
                came["r2", t, d, h].wait_recv()
        for which, mine in ((1 - xh, False), (xh, True)):
            cols = at(which * slot, slot)
            for h in range(2):
                total = own[t, h, :, cols] + r2[t, 0, h, :, cols].astype(F32) + r2[t, 1, h, :, cols].astype(F32)
                if mine:
                    own[t, h, :, cols] = total
                else:
                    s3[t, h] = total.astype(BF16)
            if not mine:
                came["r3", t] = send(s3.at[t], r3.at[t], x_at)

    def finish(t):
        came["r3", t].wait_recv()
        for h in range(2):
            total = own[t, h, :, at(xh * slot, slot)] + r3[t, h].astype(F32) + dec_bias[...]
            rebuilt[:, h, pl.ds(t * ROWS, ROWS), :] = total.reshape(8, ROWS, slot)

    steps = dict(
        relay_heads=relay_heads, project=project, hide=hide, spread_own=spread_own, spread_partner=spread_partner,
        relay_partner=relay_partner, encode=encode, sum_core=sum_core, sum_far=sum_far, sum_near=sum_near,
        activate=activate, gather_pair=gather_pair, gather_far=gather_far, gather_core=gather_core, decode=decode,
        sum_relay=sum_relay, sum_ring=sum_ring, finish=finish,
    )
    order = sorted((start + gap * t, n, t, name) for n, (name, start, gap) in enumerate(STEPS) for t in range(chunks))
    for _, _, t, name in order:
        steps[name](t)
    for copy in sent:
        copy.wait_send()


def per_device(attn_heads, out_proj, resid_pre, enc_weight, enc_bias, dec_weight, dec_bias):
    _, tokens, slot = attn_heads.shape
    width = resid_pre.shape[2]
    feats = enc_weight.shape[2]
    per_owner = tokens // LAYERS
    chunks = per_owner // ROWS
    side = LAYERS * ROWS // 2
    two = 2 * slot
    vmem, anywhere = pl.BlockSpec(memory_space=pltpu.VMEM), pl.BlockSpec(memory_space=pl.ANY)
    features, rebuilt = pl.pallas_call(
        functools.partial(kernel, chunks),
        out_shape=(
            jax.ShapeDtypeStruct((per_owner, feats), F32),
            jax.ShapeDtypeStruct((8, 2, per_owner, slot), F32),
        ),
        in_specs=[anywhere, anywhere, anywhere, anywhere, vmem, anywhere, vmem],
        out_specs=(vmem, vmem),
        scratch_shapes=[
            pltpu.VMEM((chunks, 2, 8, ROWS, 4 * slot), BF16),
            pltpu.VMEM((4 * slot, two), BF16),
            pltpu.VMEM((chunks, 2, 8, ROWS, slot), BF16),
            pltpu.VMEM((chunks, 2 * side, slot), F32),
            pltpu.VMEM((chunks, 2 * side, slot), F32),
            pltpu.VMEM((chunks, 2 * side, slot), F32),
            pltpu.VMEM((chunks, 2 * side, width), BF16),
            pltpu.VMEM((width, feats), BF16),
            pltpu.VMEM((feats, width), BF16),
            pltpu.VMEM((chunks, 2 * side, feats), F32),
            pltpu.VMEM((chunks, side, feats), F32),
            pltpu.VMEM((chunks, 2, ROWS, feats), F32),
            pltpu.VMEM((chunks, 2, 2, ROWS, feats), F32),
            pltpu.VMEM((chunks, 2, ROWS, feats), F32),
            pltpu.VMEM((chunks, ROWS, feats), F32),
            pltpu.VMEM((chunks, 2 * side, feats), BF16),
            pltpu.VMEM((chunks, side, two), F32),
            pltpu.VMEM((chunks, side, two), F32),
            pltpu.VMEM((chunks, 2, side, two), F32),
            pltpu.VMEM((chunks, 2, side, two), BF16),
            pltpu.VMEM((chunks, 2, side, two), BF16),
            pltpu.VMEM((chunks, 2, 2, side, two), BF16),
            pltpu.VMEM((chunks, 2, 2, side, two), BF16),
            pltpu.VMEM((chunks, 2, side, slot), BF16),
            pltpu.VMEM((chunks, 2, side, slot), BF16),
            pltpu.SemaphoreType.DMA((SEMS,)),
            pltpu.SemaphoreType.DMA((SEMS,)),
            pltpu.SemaphoreType.DMA((4 * chunks + 4,)),
        ],
        compiler_params=pltpu.CompilerParams(
            collective_id=0, has_side_effects=True, vmem_limit_bytes=66_000_000
        ),
        name="crosscoder",
    )(
        attn_heads.reshape(8, 2, per_owner, slot),
        out_proj[0],
        resid_pre.reshape(8, 2, per_owner, width),
        enc_weight[0],
        enc_bias.reshape(1, feats),
        dec_weight[0],
        dec_bias,
    )
    return features, rebuilt.reshape(1, tokens, slot)


def solution(mesh):
    return jax.shard_map(
        per_device,
        mesh=mesh,
        in_specs=(
            P("layer", None, "feat"),
            P("layer", "feat", None),
            P("layer", None, None),
            P("layer", None, "feat"),
            P("feat"),
            P("layer", "feat", None),
            P("layer", "feat"),
        ),
        out_specs=(P("layer", "feat"), P("layer", None, "feat")),
        check_vma=False,
    )
```

```python
import functools
import itertools

import jax
import jax.numpy as jnp
from jax import lax
from jax.experimental import pallas as pl
from jax.experimental.pallas import tpu as pltpu
from jax.sharding import PartitionSpec as P

MESH = pl.DeviceIdType.MESH
LAYERS, FEATS = 16, 8
ROWS = 16
SEMS = 256
F32, BF16 = jnp.float32, jnp.bfloat16

ORDER = (
    ("opn", 0), ("heads", 0), ("op", 0), ("relay_heads", 0), ("heads", 2), ("project", 0), ("relay_heads", 2),
    ("heads", 1), ("relay_heads", 1), ("hide", 0), ("project", 1), ("spread_own", 0), ("spread_partner", 0),
    ("relay_partner", 0), ("hide", 1), ("project", 2), ("encode0", 0), ("spread_own", 1), ("sum_core0", 0),
    ("spread_partner", 1), ("encode1", 0), ("relay_partner", 1), ("sum_far0", 0), ("sum_core1", 0), ("hide", 2),
    ("encode0", 1), ("sum_near0", 0), ("sum_far1", 0), ("sum_core0", 1), ("spread_own", 2), ("spread_partner", 2),
    ("encode1", 1), ("activate0", 0), ("sum_near1", 0), ("sum_far0", 1), ("relay_partner", 2), ("sum_core1", 1),
    ("sum_near0", 1), ("gather_pair0", 0), ("activate1", 0), ("sum_far1", 1), ("encode0", 2), ("gather_far0", 0),
    ("gather_pair1", 0), ("sum_core0", 2), ("encode1", 2), ("gather_far1", 0), ("gather_core0", 0), ("sum_near1", 1),
    ("sum_far0", 2), ("sum_core1", 2), ("activate0", 1), ("decode0", 0), ("sum_near0", 2), ("gather_pair0", 1),
    ("gather_core1", 0), ("sum_far1", 2), ("activate1", 1), ("decode", 0), ("gather_pair1", 1), ("activate0", 2),
    ("gather_far0", 1), ("sum_near1", 2), ("sum_relay0", 0), ("gather_far1", 1), ("sum_relay1", 0),
    ("gather_pair0", 2), ("gather_core0", 1), ("activate1", 2), ("gather_core1", 1), ("decode0", 1),
    ("gather_far0", 2), ("gather_pair1", 2), ("decode", 1), ("sum_ring0", 0), ("sum_ring1", 0), ("gather_core0", 2),
    ("gather_far1", 2), ("decode0", 2), ("gather_core1", 2), ("sum_relay0", 1), ("decode", 2), ("finish", 0),
    ("sum_relay0", 2), ("sum_relay1", 1), ("sum_ring0", 1), ("sum_relay1", 2), ("sum_ring0", 2), ("sum_ring1", 1),
    ("finish", 1), ("sum_ring1", 2), ("finish", 2),
)
PIECES = 2


def dot(a, b):
    return jnp.dot(a, b, preferred_element_type=F32)


def at(start, size):
    return pl.ds(pl.multiple_of(start, size), size)


def kernel(
    chunks, heads, out_proj, resid, enc, enc_bias, dec, dec_bias, features, rebuilt,
    hbuf, obuf, rbuf, psend, precv, pown, hid, encv, decv, ebuf, erecv, zfar, znear, ztot, xlrecv, coded,
    acc, s1, r1, s2, r2, s3, r3, send_sem, recv_sem, local_sem,
):
    layer, feat = lax.axis_index("layer"), lax.axis_index("feat")
    z, xl, core = layer // 4, lax.rem(layer // 2, 2), lax.rem(layer, 2)
    xh, y = feat // 4, lax.rem(feat, 4)
    yc = [lax.rem(y + k, 4) for k in range(4)]
    zc = [lax.rem(z + k, 4) for k in range(4)]
    y_at = [{"feat": xh * 4 + yc[k]} for k in range(4)]
    z_at = [{"layer": zc[k] * 4 + xl * 2 + core} for k in range(4)]
    x_at = {"feat": (1 - xh) * 4 + y}
    xl_at = {"layer": z * 4 + (1 - xl) * 2 + core}
    core_at = {"layer": z * 4 + xl * 2 + 1 - core}
    slot = out_proj.shape[0]
    half = 4 * slot
    token_rows = LAYERS * ROWS
    side = token_rows // 2
    feats = encv.shape[1]

    locals_, remotes = itertools.count(), itertools.count()
    sent, done = [], set()

    def local(src, dst):
        copy = pltpu.make_async_copy(src, dst, local_sem.at[next(locals_)])
        copy.start()
        return copy

    def send(src, dst, where):
        index = next(remotes)
        copy = pltpu.make_async_remote_copy(
            src, dst, send_sem.at[index], recv_sem.at[index], device_id=where, device_id_type=MESH
        )
        copy.start()
        sent.append(copy)
        return copy

    def first(name):
        fresh = name not in done
        done.add(name)
        return fresh

    def rows(t):
        return pl.ds(t * ROWS, ROWS)

    def group(which_z, which_xl):
        return at((core * 8 + which_z * 2 + which_xl) * ROWS, ROWS)

    def block(which_z):
        return at((core * 8 + which_z * 2) * ROWS, 2 * ROWS)

    own_cols = at(feat * slot, slot)
    partner_cols = at(((1 - xh) * 4 + y) * slot, slot)

    fetched = {}
    for t in range(chunks):
        for c in range(2):
            fetched["heads", t, c] = local(heads.at[:, c, rows(t), :], hbuf.at[t, c, :, :, at(y * slot, slot)])
    for j in range(2):
        fetched["proj", j] = local(
            out_proj.at[:, at(j * half + y * slot, slot)], obuf.at[at(y * slot, slot), pl.ds(j * slot, slot)]
        )
    for t in range(chunks):
        for c in range(2):
            fetched["resid", t, c] = local(resid.at[:, c, rows(t), own_cols], rbuf.at[t, c])
    fetched["enc"] = local(enc, encv)
    fetched["dec"] = local(dec, decv)

    barrier = pltpu.get_barrier_semaphore()
    greeted = [y_at[1], y_at[2], y_at[3], z_at[1], z_at[3], x_at, xl_at, core_at]
    for where in greeted:
        pl.semaphore_signal(barrier, inc=1, device_id=where, device_id_type=MESH)
    pl.semaphore_wait(barrier, len(greeted))

    came = {}

    def send_heads(t):
        for c, k in ((0, 1), (1, 3), (1, 1), (0, 3)):
            came["heads", t, c, k] = send(
                heads.at[:, c, rows(t), :], hbuf.at[t, c, :, :, at(y * slot, slot)], y_at[k]
            )

    def send_proj(t, which):
        for j in range(2):
            for k in which:
                came["proj", k, j] = send(
                    out_proj.at[:, at(j * half + yc[k] * slot, slot)],
                    obuf.at[at(y * slot, slot), pl.ds(j * slot, slot)],
                    y_at[k],
                )

    def relay_heads(t):
        for c, k, back in ((0, 1, 3), (1, 3, 1)):
            came["heads", t, c, k].wait_recv()
            part = hbuf.at[t, c, :, :, at(yc[back] * slot, slot)]
            came["heads2", t, c] = send(part, part, y_at[k])

    def project(t):
        if first("project"):
            for j in range(2):
                fetched["proj", j].wait()
            for k in (1, 3, 2):
                for j in range(2):
                    came["proj", k, j].wait_recv()
        for c in range(2):
            fetched["heads", t, c].wait()
            fetched["resid", t, c].wait()
        for c, k in ((1, 1), (0, 3)):
            came["heads", t, c, k].wait_recv()
        for c in range(2):
            came["heads2", t, c].wait_recv()
        lhs = hbuf[t].reshape(token_rows, half)
        psend[t] = dot(lhs, obuf[:, at((1 - xh) * slot, slot)])
        came["part", t] = send(psend.at[t], precv.at[t], x_at)
        pown[t] = dot(lhs, obuf[:, at(xh * slot, slot)])

    def ring_send(name, t, cols):
        for h, k in ((0, 1), (1, 3), (1, 1), (0, 3)):
            part = hid.at[t, pl.ds(h * side, side), cols]
            came[name, t, h, k] = send(part, part, y_at[k])

    def ring_relay(name, t, which_xh):
        for h, k, back in ((0, 1, 3), (1, 3, 1)):
            came[name, t, h, k].wait_recv()
            part = hid.at[t, pl.ds(h * side, side), at((which_xh * 4 + yc[back]) * slot, slot)]
            came[name + "2", t, h] = send(part, part, y_at[k])

    def ring_wait(name, t):
        for h, k in ((1, 1), (0, 3)):
            came[name, t, h, k].wait_recv()
        for h in range(2):
            came[name + "2", t, h].wait_recv()

    def hide(t):
        came["part", t].wait_recv()
        projected = pown[t] + precv[t]
        residual = rbuf[t].reshape(token_rows, slot).astype(F32)
        hid[t, :, own_cols] = (residual + projected).astype(BF16)
        part = hid.at[t, :, own_cols]
        came["pair", t] = send(part, part, x_at)
        ring_send("ring", t, own_cols)

    def spread_own(t):
        ring_relay("ring", t, xh)

    def spread_partner(t):
        came["pair", t].wait_recv()
        ring_send("other", t, partner_cols)

    def relay_partner(t):
        ring_relay("other", t, 1 - xh)

    width = feats // PIECES

    def encode(t, q):
        if first("encode"):
            fetched["enc"].wait()
        if q == 0:
            ring_wait("ring", t)
            ring_wait("other", t)
        for part in range(2):
            start = q * width + part * (width // 2)

            def tile(n, carry):
                cols = at(start + n * 256, 256)
                ebuf[t, :, cols] = dot(hid[t], encv[:, cols])
                return carry

            lax.fori_loop(0, width // 512, tile, 0)
            cols = pl.ds(start, width // 2)
            came["core", t, q, part] = send(
                ebuf.at[t, at((1 - core) * side, side), cols], erecv.at[t, :, cols], core_at
            )

    def sum_core(t, q):
        mine = at(core * side, side)
        for part in range(2):
            cols = pl.ds(q * width + part * (width // 2), width // 2)
            came["core", t, q, part].wait_recv()
            ebuf[t, mine, cols] = ebuf[t, mine, cols] + erecv[t, :, cols]
        cols = pl.ds(q * width, width)
        for name, which, kind, to, k in (
            ("zfar", (zc[2], xl), (0,), zfar.at[t, 0], 1),
            ("zfar", (zc[2], 1 - xl), (1,), zfar.at[t, 1], 3),
            ("znear", (zc[1], 1 - xl), (0, 1), znear.at[t, 0, 1], 1),
            ("znear", (zc[3], xl), (1, 0), znear.at[t, 1, 0], 3),
        ):
            came[name, t, q, *kind] = send(ebuf.at[t, group(*which), cols], to.at[:, cols], z_at[k])

    def sum_far(t, q):
        cols = pl.ds(q * width, width)
        for d, here, k in ((0, group(zc[1], xl), 1), (1, group(zc[3], 1 - xl), 3)):
            came["zfar", t, q, d].wait_recv()
            ebuf[t, here, cols] = ebuf[t, here, cols] + zfar[t, d, :, cols]
            came["znear", t, q, d, d] = send(ebuf.at[t, here, cols], znear.at[t, d, d, :, cols], z_at[k])

    def sum_near(t, q):
        cols = pl.ds(q * width, width)
        for kind, which in ((1, 1 - xl), (0, xl)):
            came["znear", t, q, 0, kind].wait_recv()
            came["znear", t, q, 1, kind].wait_recv()
            ztot[t, kind, :, cols] = (
                ebuf[t, group(z, which), cols] + znear[t, 0, kind, :, cols] + znear[t, 1, kind, :, cols]
            )
            if kind == 1:
                came["xl", t, q] = send(ztot.at[t, 1, :, cols], xlrecv.at[t, :, cols], xl_at)

    def activate(t, q):
        cols = pl.ds(q * width, width)
        came["xl", t, q].wait_recv()
        active = jnp.maximum(ztot[t, 0, :, cols] + xlrecv[t, :, cols] + enc_bias[:, cols], 0.0)
        features[pl.ds(t * ROWS, ROWS), cols] = active
        here = group(z, xl)
        coded[t, here, cols] = active.astype(BF16)
        part = coded.at[t, here, cols]
        came["cpair", t, q] = send(part, part, xl_at)
        came["cown", t, q, 1] = send(part, part, z_at[1])
        came["cown", t, q, 3] = send(part, part, z_at[3])

    def gather_pair(t, q):
        cols = pl.ds(q * width, width)
        came["cpair", t, q].wait_recv()
        part = coded.at[t, group(z, 1 - xl), cols]
        came["cother", t, q, 1] = send(part, part, z_at[1])
        came["cother", t, q, 3] = send(part, part, z_at[3])
        part = coded.at[t, block(z), cols]
        came["ccore", t, q, 0] = send(part, part, core_at)

    def gather_far(t, q):
        cols = pl.ds(q * width, width)
        came["cown", t, q, 1].wait_recv()
        part = coded.at[t, group(zc[3], xl), cols]
        came["cown2", t, q] = send(part, part, z_at[1])
        came["cother", t, q, 3].wait_recv()
        part = coded.at[t, group(zc[1], 1 - xl), cols]
        came["cother2", t, q] = send(part, part, z_at[3])
        came["cother", t, q, 1].wait_recv()
        part = coded.at[t, block(zc[3]), cols]
        came["ccore", t, q, 3] = send(part, part, core_at)
        came["cown", t, q, 3].wait_recv()
        part = coded.at[t, block(zc[1]), cols]
        came["ccore", t, q, 1] = send(part, part, core_at)

    def gather_core(t, q):
        came["cown2", t, q].wait_recv()
        came["cother2", t, q].wait_recv()
        part = coded.at[t, block(zc[2]), pl.ds(q * width, width)]
        came["ccore", t, q, 2] = send(part, part, core_at)

    def to_cols(j, which):
        return at((xh if j else 1 - xh) * half + yc[which] * slot, slot)

    def decode_early(t, q):
        if first("decode"):
            fetched["dec"].wait()
        for k in range(4):
            came["ccore", t, q, k].wait_recv()
        depth = pl.ds(q * width, width)

        def tile(n, carry):
            cols = at(n * slot, slot)
            out = dot(coded[t, :, depth], decv[depth, cols])
            acc[t, :, cols] = out if q == 0 else acc[t, :, cols] + out
            return carry

        lax.fori_loop(0, 8, tile, 0)

    def decode(t):
        q = PIECES - 1
        for k in range(4):
            came["ccore", t, q, k].wait_recv()
        depth = pl.ds(q * width, width)
        low, high = pl.ds(0, side), pl.ds(side, side)

        def tile(j, which):
            cols = to_cols(j, which)
            return cols, acc[t, :, cols] + dot(coded[t, :, depth], decv[depth, cols])

        for j in range(2):
            cols, out = tile(j, 2)
            s1[t, j] = out.astype(BF16).reshape(2, side, slot)
            came["r1", t, j, 0] = send(s1.at[t, j, 0], r1.at[t, j, 0], y_at[1])
            came["r1", t, j, 1] = send(s1.at[t, j, 1], r1.at[t, j, 1], y_at[3])
            cols, out = tile(j, 1)
            acc[t, low, cols] = out[:side]
            s2[t, j, 0, 1] = out[side:].astype(BF16)
            came["r2", t, j, 0, 1] = send(s2.at[t, j, 0, 1], r2.at[t, j, 0, 1], y_at[1])
            cols, out = tile(j, 3)
            s2[t, j, 1, 0] = out[:side].astype(BF16)
            acc[t, high, cols] = out[side:]
            came["r2", t, j, 1, 0] = send(s2.at[t, j, 1, 0], r2.at[t, j, 1, 0], y_at[3])
        for j in range(2):
            cols, out = tile(j, 0)
            acc[t, :, cols] = out

    def sum_relay(t, j):
        for d, k, h in ((0, 1, pl.ds(0, side)), (1, 3, pl.ds(side, side))):
            came["r1", t, j, d].wait_recv()
            s2[t, j, d, d] = (acc[t, h, to_cols(j, k)] + r1[t, j, d].astype(F32)).astype(BF16)
            came["r2", t, j, d, d] = send(s2.at[t, j, d, d], r2.at[t, j, d, d], y_at[k])

    def sum_ring(t, j):
        for d in range(2):
            for h in range(2):
                came["r2", t, j, d, h].wait_recv()
        cols = to_cols(j, 0)
        for h in range(2):
            here = pl.ds(h * side, side)
            total = acc[t, here, cols] + r2[t, j, 0, h].astype(F32) + r2[t, j, 1, h].astype(F32)
            if j == 1:
                acc[t, here, cols] = total
            else:
                s3[t, h] = total.astype(BF16)
        if j == 0:
            came["r3", t] = send(s3.at[t], r3.at[t], x_at)

    def finish(t):
        came["r3", t].wait_recv()
        cols = to_cols(1, 0)
        for h in range(2):
            total = acc[t, pl.ds(h * side, side), cols] + r3[t, h].astype(F32) + dec_bias[...]
            rebuilt[:, h, pl.ds(t * ROWS, ROWS), :] = total.reshape(8, ROWS, slot)

    steps = dict(
        heads=send_heads, op=functools.partial(send_proj, which=(2,)), opn=functools.partial(send_proj, which=(1, 3)),
        relay_heads=relay_heads, project=project, hide=hide, spread_own=spread_own, spread_partner=spread_partner,
        relay_partner=relay_partner, decode=decode, finish=finish,
    )
    for q in range(PIECES):
        for step in (encode, sum_core, sum_far, sum_near, activate, gather_pair, gather_far, gather_core):
            steps[f"{step.__name__}{q}"] = functools.partial(step, q=q)
    for q in range(PIECES - 1):
        steps[f"decode{q}"] = functools.partial(decode_early, q=q)
    for j in range(2):
        steps[f"sum_relay{j}"] = functools.partial(sum_relay, j=j)
        steps[f"sum_ring{j}"] = functools.partial(sum_ring, j=j)
    for name, t in ORDER:
        steps[name](t)
    for copy in sent:
        copy.wait_send()


def per_device(attn_heads, out_proj, resid_pre, enc_weight, enc_bias, dec_weight, dec_bias):
    _, tokens, slot = attn_heads.shape
    width = resid_pre.shape[2]
    feats = enc_weight.shape[2]
    per_owner = tokens // LAYERS
    chunks = per_owner // ROWS
    side = LAYERS * ROWS // 2
    two = 2 * slot
    vmem, anywhere = pl.BlockSpec(memory_space=pltpu.VMEM), pl.BlockSpec(memory_space=pl.ANY)
    features, rebuilt = pl.pallas_call(
        functools.partial(kernel, chunks),
        out_shape=(
            jax.ShapeDtypeStruct((per_owner, feats), F32),
            jax.ShapeDtypeStruct((8, 2, per_owner, slot), F32),
        ),
        in_specs=[anywhere, anywhere, anywhere, anywhere, vmem, anywhere, vmem],
        out_specs=(vmem, vmem),
        scratch_shapes=[
            pltpu.VMEM((chunks, 2, 8, ROWS, 4 * slot), BF16),
            pltpu.VMEM((4 * slot, two), BF16),
            pltpu.VMEM((chunks, 2, 8, ROWS, slot), BF16),
            pltpu.VMEM((chunks, 2 * side, slot), F32),
            pltpu.VMEM((chunks, 2 * side, slot), F32),
            pltpu.VMEM((chunks, 2 * side, slot), F32),
            pltpu.VMEM((chunks, 2 * side, width), BF16),
            pltpu.VMEM((width, feats), BF16),
            pltpu.VMEM((feats, width), BF16),
            pltpu.VMEM((chunks, 2 * side, feats), F32),
            pltpu.VMEM((chunks, side, feats), F32),
            pltpu.VMEM((chunks, 2, ROWS, feats), F32),
            pltpu.VMEM((chunks, 2, 2, ROWS, feats), F32),
            pltpu.VMEM((chunks, 2, ROWS, feats), F32),
            pltpu.VMEM((chunks, ROWS, feats), F32),
            pltpu.VMEM((chunks, 2 * side, feats), BF16),
            pltpu.VMEM((chunks, 2 * side, width), F32),
            pltpu.VMEM((chunks, 2, 2, side, slot), BF16),
            pltpu.VMEM((chunks, 2, 2, side, slot), BF16),
            pltpu.VMEM((chunks, 2, 2, 2, side, slot), BF16),
            pltpu.VMEM((chunks, 2, 2, 2, side, slot), BF16),
            pltpu.VMEM((chunks, 2, side, slot), BF16),
            pltpu.VMEM((chunks, 2, side, slot), BF16),
            pltpu.SemaphoreType.DMA((SEMS,)),
            pltpu.SemaphoreType.DMA((SEMS,)),
            pltpu.SemaphoreType.DMA((4 * chunks + 4,)),
        ],
        compiler_params=pltpu.CompilerParams(
            collective_id=0, has_side_effects=True, vmem_limit_bytes=66_000_000
        ),
        name="crosscoder",
    )(
        attn_heads.reshape(8, 2, per_owner, slot),
        out_proj[0],
        resid_pre.reshape(8, 2, per_owner, width),
        enc_weight[0],
        enc_bias.reshape(1, feats),
        dec_weight[0],
        dec_bias,
    )
    return features, rebuilt.reshape(1, tokens, slot)


def solution(mesh):
    return jax.shard_map(
        per_device,
        mesh=mesh,
        in_specs=(
            P("layer", None, "feat"),
            P("layer", "feat", None),
            P("layer", None, None),
            P("layer", None, "feat"),
            P("feat"),
            P("layer", "feat", None),
            P("layer", "feat"),
        ),
        out_specs=(P("layer", "feat"), P("layer", None, "feat")),
        check_vma=False,
    )
```

```python
import functools
import itertools

import jax
import jax.numpy as jnp
from jax import lax
from jax.experimental import pallas as pl
from jax.experimental.pallas import tpu as pltpu
from jax.sharding import PartitionSpec as P

MESH = pl.DeviceIdType.MESH
LAYERS, FEATS = 16, 8
ROWS = 16
SEMS = 256
F32, BF16 = jnp.float32, jnp.bfloat16

ORDER = (
    (2, 0), (0, 0), (1, 0), (3, 0), (0, 2), (4, 0), (0, 1), (3, 2), (3, 1), (5, 0), (6, 0), (4, 1), (8, 0), (9, 0),
    (7, 0), (10, 0), (5, 1), (6, 1), (4, 2), (11, 0), (8, 1), (9, 1), (7, 1), (12, 0), (13, 0), (5, 2), (10, 1),
    (14, 0), (6, 2), (15, 0), (8, 2), (11, 1), (9, 2), (12, 1), (7, 2), (16, 0), (17, 0), (13, 1), (10, 2), (14, 1),
    (19, 0), (18, 0), (11, 2), (12, 2), (20, 0), (13, 2), (16, 1), (21, 0), (15, 1), (22, 0), (14, 2), (17, 1),
    (18, 1), (15, 2), (23, 0), (16, 2), (20, 1), (19, 1), (17, 2), (18, 2), (22, 1), (25, 0), (21, 1), (20, 2),
    (19, 2), (24, 0), (23, 1), (22, 2), (26, 0), (27, 0), (21, 2), (24, 1), (23, 2), (26, 1), (28, 0), (24, 2),
    (25, 1), (26, 2), (25, 2), (27, 1), (28, 1), (27, 2), (28, 2),
)
PIECES, PARTS = 2, 2


def dot(a, b):
    return jnp.dot(a, b, preferred_element_type=F32)


def at(start, size):
    return pl.ds(pl.multiple_of(start, size), size)


def kernel(
    chunks, heads, out_proj, resid, enc, enc_bias, dec, dec_bias, features, rebuilt,
    hbuf, obuf, rbuf, psend, precv, pown, hid, encv, decv, ebuf, erecv, zsend, zrecv, ztot, xlrecv, coded,
    acc, s1, r1, s2, r2, s3, r3, fout, rout, send_sem, recv_sem, local_sem,
):
    layer, feat = lax.axis_index("layer"), lax.axis_index("feat")
    z, xl, core = layer // 4, lax.rem(layer // 2, 2), lax.rem(layer, 2)
    xh, y = feat // 4, lax.rem(feat, 4)
    yc = [lax.rem(y + k, 4) for k in range(4)]
    zc = [lax.rem(z + k, 4) for k in range(4)]
    y_at = [{"feat": xh * 4 + yc[k]} for k in range(4)]
    z_at = [{"layer": zc[k] * 4 + xl * 2 + core} for k in range(4)]
    x_at = {"feat": (1 - xh) * 4 + y}
    xl_at = {"layer": z * 4 + (1 - xl) * 2 + core}
    core_at = {"layer": z * 4 + xl * 2 + 1 - core}
    slot = out_proj.shape[0]
    half = 4 * slot
    token_rows = LAYERS * ROWS
    side = token_rows // 2
    feats = encv.shape[1]

    locals_, remotes = itertools.count(), itertools.count()
    sent, out, done = [], [], set()

    def local(src, dst):
        copy = pltpu.make_async_copy(src, dst, local_sem.at[next(locals_)])
        copy.start()
        return copy

    def send(src, dst, where):
        index = next(remotes)
        copy = pltpu.make_async_remote_copy(
            src, dst, send_sem.at[index], recv_sem.at[index], device_id=where, device_id_type=MESH
        )
        copy.start()
        sent.append(copy)
        return copy

    def first(name):
        fresh = name not in done
        done.add(name)
        return fresh

    def rows(t):
        return pl.ds(t * ROWS, ROWS)

    def group(which_z, which_xl):
        return at((core * 8 + which_z * 2 + which_xl) * ROWS, ROWS)

    def block(which_z):
        return at((core * 8 + which_z * 2) * ROWS, 2 * ROWS)

    own_cols = at(feat * slot, slot)
    partner_cols = at(((1 - xh) * 4 + y) * slot, slot)

    def to_cols(j, which):
        return at((xh if j else 1 - xh) * half + yc[which] * slot, slot)

    fetched = {}
    for t in range(chunks):
        for c in range(2):
            fetched["heads", t, c] = local(heads.at[:, c, rows(t), :], hbuf.at[t, c, :, :, at(y * slot, slot)])
    for j in range(2):
        fetched["proj", j] = local(
            out_proj.at[:, to_cols(j, 0)], obuf.at[at(y * slot, slot), pl.ds(j * slot, slot)]
        )
    for t in range(chunks):
        for c in range(2):
            fetched["resid", t, c] = local(resid.at[:, c, rows(t), own_cols], rbuf.at[t, c])
    fetched["enc"] = local(enc, encv)
    fetched["dec"] = local(dec, decv)

    barrier = pltpu.get_barrier_semaphore()
    greeted = [*y_at[1:], *z_at[1:], x_at, xl_at, core_at]
    for where in greeted:
        pl.semaphore_signal(barrier, inc=1, device_id=where, device_id_type=MESH)
    pl.semaphore_wait(barrier, len(greeted))

    came = {}

    def send_heads(t):
        for c, k in ((0, 1), (1, 3), (1, 1), (0, 3)):
            came["heads", t, c, k] = send(
                heads.at[:, c, rows(t), :], hbuf.at[t, c, :, :, at(y * slot, slot)], y_at[k]
            )

    def send_proj(t, which):
        for j in range(2):
            for k in which:
                came["proj", k, j] = send(
                    out_proj.at[:, to_cols(j, k)],
                    obuf.at[at(y * slot, slot), pl.ds(j * slot, slot)],
                    y_at[k],
                )

    def relay_heads(t):
        for c, k, back in ((0, 1, 3), (1, 3, 1)):
            came["heads", t, c, k].wait_recv()
            part = hbuf.at[t, c, :, :, at(yc[back] * slot, slot)]
            came["heads2", t, c] = send(part, part, y_at[k])

    def project(t):
        if first("project"):
            for j in range(2):
                fetched["proj", j].wait()
            for k in (1, 3, 2):
                for j in range(2):
                    came["proj", k, j].wait_recv()
        for c in range(2):
            fetched["heads", t, c].wait()
            fetched["resid", t, c].wait()
        for c, k in ((1, 1), (0, 3)):
            came["heads", t, c, k].wait_recv()
        for c in range(2):
            came["heads2", t, c].wait_recv()
        lhs = hbuf[t].reshape(token_rows, half)
        value = dot(lhs, obuf[...])
        psend[t] = value[:, :slot].reshape(2, side, slot)
        for h in range(2):
            came["part", t, h] = send(psend.at[t, h], precv.at[t, h], x_at)
        pown[t] = value[:, slot:].reshape(2, side, slot)

    def ring_send(name, t, h, cols):
        for k in (1, 3):
            part = hid.at[t, pl.ds(h * side, side), cols]
            came[name, t, h, k] = send(part, part, y_at[k])

    def ring_relay(name, t, which_xh):
        for h, k, back in ((0, 1, 3), (1, 3, 1)):
            came[name, t, h, k].wait_recv()
            part = hid.at[t, pl.ds(h * side, side), at((which_xh * 4 + yc[back]) * slot, slot)]
            came[name + "2", t, h] = send(part, part, y_at[k])

    def ring_wait(name, t):
        for h, k in ((1, 1), (0, 3)):
            came[name, t, h, k].wait_recv()
        for h in range(2):
            came[name + "2", t, h].wait_recv()

    def hide(t, h):
        came["part", t, h].wait_recv()
        projected = pown[t, h] + precv[t, h]
        residual = rbuf[t, h].reshape(side, slot).astype(F32)
        here = pl.ds(h * side, side)
        hid[t, here, own_cols] = (residual + projected).astype(BF16)
        part = hid.at[t, here, own_cols]
        came["pair", t, h] = send(part, part, x_at)
        ring_send("ring", t, h, own_cols)

    def spread_own(t):
        ring_relay("ring", t, xh)

    def spread_partner(t, h):
        came["pair", t, h].wait_recv()
        ring_send("other", t, h, partner_cols)

    def relay_partner(t):
        ring_relay("other", t, 1 - xh)

    width = feats // PIECES
    tile_width = width // PARTS

    def encode(t, q):
        if first("encode"):
            fetched["enc"].wait()
        if q == 0:
            ring_wait("ring", t)
            ring_wait("other", t)
        cols = pl.ds(q * width, width)
        ebuf[t, :, cols] = dot(hid[t], encv[:, cols])
        for part in range(PARTS):
            cols = pl.ds(q * width + part * tile_width, tile_width)
            came["core", t, q, part] = send(
                ebuf.at[t, at((1 - core) * side, side), cols], erecv.at[t, :, cols], core_at
            )

    def sum_core(t, q):
        cols = pl.ds(q * width, width)
        for part in range(PARTS):
            came["core", t, q, part].wait_recv()
        for k in (2, 1, 3, 0):
            total = ebuf[t, block(zc[k]), cols] + erecv[t, at(zc[k] * 2 * ROWS, 2 * ROWS), cols]
            if k:
                zsend[t, k - 1, :, cols] = total.astype(BF16)
                came["zsum", t, q, k] = send(zsend.at[t, k - 1, :, cols], zrecv.at[t, k - 1, :, cols], z_at[k])
            else:
                ebuf[t, block(z), cols] = total

    def sum_near(t, q):
        cols = pl.ds(q * width, width)
        for k in (1, 3, 2):
            came["zsum", t, q, k].wait_recv()
        for kind, which in ((1, 1 - xl), (0, xl)):
            total = ebuf[t, group(z, which), cols]
            for k in range(3):
                total = total + zrecv[t, k, at(which * ROWS, ROWS), cols].astype(F32)
            ztot[t, kind, :, cols] = total
            if kind == 1:
                came["xl", t, q] = send(ztot.at[t, 1, :, cols], xlrecv.at[t, :, cols], xl_at)

    def activate(t, q):
        cols = pl.ds(q * width, width)
        came["xl", t, q].wait_recv()
        active = jnp.maximum(ztot[t, 0, :, cols] + xlrecv[t, :, cols] + enc_bias[:, cols], 0.0)
        here = group(z, xl)
        coded[t, here, cols] = active.astype(BF16)
        part = coded.at[t, here, cols]
        came["cpair", t, q] = send(part, part, xl_at)
        for k in (2, 1, 3):
            came["cown", t, q, k] = send(part, part, z_at[k])
        fout[t, :, cols] = active
        out.append(local(fout.at[t, :, cols], features.at[rows(t), cols]))

    def gather_pair(t, q):
        cols = pl.ds(q * width, width)
        came["cpair", t, q].wait_recv()
        part = coded.at[t, group(z, 1 - xl), cols]
        for k in (2, 1, 3):
            came["cother", t, q, k] = send(part, part, z_at[k])
        part = coded.at[t, block(z), cols]
        came["ccore", t, q, 0] = send(part, part, core_at)

    def gather_core(t, q):
        for k in (1, 3, 2):
            came["cown", t, q, k].wait_recv()
            came["cother", t, q, k].wait_recv()
            part = coded.at[t, block(zc[4 - k]), pl.ds(q * width, width)]
            came["ccore", t, q, k] = send(part, part, core_at)

    def decode(t):
        if first("decode"):
            fetched["dec"].wait()
        for q in range(PIECES):
            for k in range(4):
                came["ccore", t, q, k].wait_recv()
        low, high = pl.ds(0, side), pl.ds(side, side)
        for j in range(2):
            cols = at((xh if j else 1 - xh) * half, half)
            acc[t, :, cols] = dot(coded[t], decv[:, cols])
            s1[t, j] = acc[t, :, to_cols(j, 2)].astype(BF16).reshape(2, side, slot)
            s2[t, j, 0, 1] = acc[t, high, to_cols(j, 1)].astype(BF16)
            s2[t, j, 1, 0] = acc[t, low, to_cols(j, 3)].astype(BF16)
            came["r1", t, j, 0] = send(s1.at[t, j, 0], r1.at[t, j, 0], y_at[1])
            came["r1", t, j, 1] = send(s1.at[t, j, 1], r1.at[t, j, 1], y_at[3])
            came["r2", t, j, 0, 1] = send(s2.at[t, j, 0, 1], r2.at[t, j, 0, 1], y_at[1])
            came["r2", t, j, 1, 0] = send(s2.at[t, j, 1, 0], r2.at[t, j, 1, 0], y_at[3])

    def sum_relay(t, j):
        for d, k, h in ((0, 1, pl.ds(0, side)), (1, 3, pl.ds(side, side))):
            came["r1", t, j, d].wait_recv()
            s2[t, j, d, d] = (acc[t, h, to_cols(j, k)] + r1[t, j, d].astype(F32)).astype(BF16)
            came["r2", t, j, d, d] = send(s2.at[t, j, d, d], r2.at[t, j, d, d], y_at[k])

    def sum_ring(t, j):
        for d in range(2):
            for h in range(2):
                came["r2", t, j, d, h].wait_recv()
        cols = to_cols(j, 0)
        for h in range(2):
            here = pl.ds(h * side, side)
            total = acc[t, here, cols] + r2[t, j, 0, h].astype(F32) + r2[t, j, 1, h].astype(F32)
            if j == 1:
                acc[t, here, cols] = total
            else:
                s3[t, h] = total
        if j == 0:
            came["r3", t] = send(s3.at[t], r3.at[t], x_at)

    def finish(t):
        came["r3", t].wait_recv()
        cols = to_cols(1, 0)
        for h in range(2):
            total = acc[t, pl.ds(h * side, side), cols] + r3[t, h] + dec_bias[...]
            rout[t, h] = total.reshape(8, ROWS, slot)
            out.append(local(rout.at[t, h], rebuilt.at[:, h, rows(t), :]))

    def each(step, count):
        return [functools.partial(lambda t, n: step(t, n), n=n) for n in range(count)]

    steps = [
        send_heads, lambda t: send_proj(t, (2,)), lambda t: send_proj(t, (1, 3)), relay_heads, project, *each(hide, 2),
        spread_own, *each(spread_partner, 2), relay_partner, *each(encode, PIECES), *each(sum_core, PIECES),
        *each(sum_near, PIECES), *each(activate, PIECES), *each(gather_pair, PIECES), *each(gather_core, PIECES),
        decode, *each(sum_relay, 2), *each(sum_ring, 2), finish,
    ]
    for step, t in ORDER:
        steps[step](t)
    for copy in out:
        copy.wait()
    for copy in sent:
        copy.wait_send()


def per_device(attn_heads, out_proj, resid_pre, enc_weight, enc_bias, dec_weight, dec_bias):
    _, tokens, slot = attn_heads.shape
    width = resid_pre.shape[2]
    feats = enc_weight.shape[2]
    per_owner = tokens // LAYERS
    chunks = per_owner // ROWS
    side = LAYERS * ROWS // 2
    two = 2 * slot
    vmem, anywhere = pl.BlockSpec(memory_space=pltpu.VMEM), pl.BlockSpec(memory_space=pl.ANY)
    features, rebuilt = pl.pallas_call(
        functools.partial(kernel, chunks),
        out_shape=(
            jax.ShapeDtypeStruct((per_owner, feats), F32),
            jax.ShapeDtypeStruct((8, 2, per_owner, slot), F32),
        ),
        in_specs=[anywhere, anywhere, anywhere, anywhere, vmem, anywhere, vmem],
        out_specs=(anywhere, anywhere),
        scratch_shapes=[
            pltpu.VMEM((chunks, 2, 8, ROWS, 4 * slot), BF16),
            pltpu.VMEM((4 * slot, two), BF16),
            pltpu.VMEM((chunks, 2, 8, ROWS, slot), BF16),
            pltpu.VMEM((chunks, 2, side, slot), F32),
            pltpu.VMEM((chunks, 2, side, slot), F32),
            pltpu.VMEM((chunks, 2, side, slot), F32),
            pltpu.VMEM((chunks, 2 * side, width), BF16),
            pltpu.VMEM((width, feats), BF16),
            pltpu.VMEM((feats, width), BF16),
            pltpu.VMEM((chunks, 2 * side, feats), F32),
            pltpu.VMEM((chunks, side, feats), F32),
            pltpu.VMEM((chunks, 3, 2 * ROWS, feats), BF16),
            pltpu.VMEM((chunks, 3, 2 * ROWS, feats), BF16),
            pltpu.VMEM((chunks, 2, ROWS, feats), F32),
            pltpu.VMEM((chunks, ROWS, feats), F32),
            pltpu.VMEM((chunks, 2 * side, feats), BF16),
            pltpu.VMEM((chunks, 2 * side, width), F32),
            pltpu.VMEM((chunks, 2, 2, side, slot), BF16),
            pltpu.VMEM((chunks, 2, 2, side, slot), BF16),
            pltpu.VMEM((chunks, 2, 2, 2, side, slot), BF16),
            pltpu.VMEM((chunks, 2, 2, 2, side, slot), BF16),
            pltpu.VMEM((chunks, 2, side, slot), F32),
            pltpu.VMEM((chunks, 2, side, slot), F32),
            pltpu.VMEM((chunks, ROWS, feats), F32),
            pltpu.VMEM((chunks, 2, 8, ROWS, slot), F32),
            pltpu.SemaphoreType.DMA((SEMS,)),
            pltpu.SemaphoreType.DMA((SEMS,)),
            pltpu.SemaphoreType.DMA((8 * chunks + 4,)),
        ],
        compiler_params=pltpu.CompilerParams(
            collective_id=0, has_side_effects=True, vmem_limit_bytes=66_000_000
        ),
        name="crosscoder",
    )(
        attn_heads.reshape(8, 2, per_owner, slot),
        out_proj[0],
        resid_pre.reshape(8, 2, per_owner, width),
        enc_weight[0],
        enc_bias.reshape(1, feats),
        dec_weight[0],
        dec_bias,
    )
    return features, rebuilt.reshape(1, tokens, slot)


def solution(mesh):
    return jax.shard_map(
        per_device,
        mesh=mesh,
        in_specs=(
            P("layer", None, "feat"),
            P("layer", "feat", None),
            P("layer", None, None),
            P("layer", None, "feat"),
            P("feat"),
            P("layer", "feat", None),
            P("layer", "feat"),
        ),
        out_specs=(P("layer", "feat"), P("layer", None, "feat")),
        check_vma=False,
    )
```

```python
import functools
import math

import jax
import jax.numpy as jnp
from jax import lax
from jax.experimental import pallas as pl
from jax.experimental.pallas import tpu as pltpu
from jax.sharding import PartitionSpec as P

MESH = pl.DeviceIdType.MESH
LAYERS, FEATS = 16, 8
ROWS = 16
ARRIVALS, FETCHES = 97, 7
F32, BF16 = jnp.float32, jnp.bfloat16

ORDER = (
    (0, 0), (2, 0), (1, 0), (3, 0), (0, 1), (0, 2), (4, 0), (3, 1), (5, 0), (6, 0), (4, 1), (8, 0), (3, 2), (9, 0),
    (7, 0), (10, 0), (5, 1), (6, 1), (4, 2), (11, 0), (8, 1), (12, 0), (9, 1), (7, 1), (13, 0), (5, 2), (10, 1),
    (6, 2), (14, 0), (8, 2), (15, 0), (11, 1), (9, 2), (12, 1), (7, 2), (17, 0), (10, 2), (16, 0), (13, 1), (14, 1),
    (11, 2), (12, 2), (18, 0), (19, 0), (13, 2), (15, 1), (14, 2), (20, 0), (16, 1), (17, 1), (15, 2), (21, 0),
    (18, 1), (16, 2), (19, 1), (17, 2), (23, 0), (22, 0), (20, 1), (18, 2), (21, 1), (25, 0), (19, 2), (24, 0),
    (20, 2), (22, 1), (21, 2), (24, 1), (22, 2), (23, 1), (26, 0), (24, 2), (23, 2), (25, 1), (26, 1), (25, 2),
    (26, 2),
)
PIECES, PARTS = 2, 2


def dot(a, b):
    return jnp.dot(a, b, preferred_element_type=F32)


def at(start, size):
    return pl.ds(pl.multiple_of(start, size), size)


def kernel(
    chunks, heads, out_proj, resid, enc, enc_bias, dec, dec_bias, features, rebuilt,
    hbuf, obuf, rbuf, psend, precv, pown, hid, encv, decv, ebuf, erecv, zsend, zrecv, ztot, xlrecv, coded,
    acc, s1, r1, s2, r2, s3, r3, s4, r4, fout, rout, send_sem, recv_sem, local_sem,
):
    layer, feat = lax.axis_index("layer"), lax.axis_index("feat")
    z, xl, core = layer // 4, lax.rem(layer // 2, 2), lax.rem(layer, 2)
    xh, y = feat // 4, lax.rem(feat, 4)
    yc = [lax.rem(y + k, 4) for k in range(4)]
    zc = [lax.rem(z + k, 4) for k in range(4)]
    y_at = [{"feat": xh * 4 + yc[k]} for k in range(4)]
    z_at = [{"layer": zc[k] * 4 + xl * 2 + core} for k in range(4)]
    x_at = {"feat": (1 - xh) * 4 + y}
    xl_at = {"layer": z * 4 + (1 - xl) * 2 + core}
    core_at = {"layer": z * 4 + xl * 2 + 1 - core}
    slot = out_proj.shape[0]
    half = 4 * slot
    token_rows = LAYERS * ROWS
    side = token_rows // 2
    feats = encv.shape[1]

    done, fetching, arriving, sent = set(), {}, {}, {}

    def expect(groups, sems, key, ref):
        index, size = groups.get(key, (len(groups), 0))
        assert index < sems.shape[0]
        groups[key] = index, size + math.prod(ref.shape) * ref.dtype.itemsize
        return sems.at[index]

    def settle(groups, sems, key):
        index, size = groups[key]
        view = encv.at[pl.ds(0, size // (2 * encv.shape[1]))]
        pltpu.make_async_copy(view, view, sems.at[index]).wait()

    def local(src, dst, *key):
        pltpu.make_async_copy(src, dst, expect(fetching, local_sem, key, dst)).start()

    def fetched(*key):
        settle(fetching, local_sem, key)

    def send(src, dst, where, t, *key):
        pltpu.make_async_remote_copy(
            src, dst, expect(sent, send_sem, t, src), expect(arriving, recv_sem, (t, *key), dst),
            device_id=where, device_id_type=MESH,
        ).start()

    def arrived(*key):
        settle(arriving, recv_sem, key)

    def first(name):
        fresh = name not in done
        done.add(name)
        return fresh

    def rows(t):
        return pl.ds(t * ROWS, ROWS)

    def group(which_z, which_xl):
        return at((core * 8 + which_z * 2 + which_xl) * ROWS, ROWS)

    def block(which_z):
        return at((core * 8 + which_z * 2) * ROWS, 2 * ROWS)

    own_cols = at(feat * slot, slot)
    partner_cols = at(((1 - xh) * 4 + y) * slot, slot)

    def to_cols(j, which):
        return at((xh if j else 1 - xh) * half + yc[which] * slot, slot)

    for t in range(chunks):
        for c in range(2):
            local(heads.at[:, c, rows(t), :], hbuf.at[t, c, :, :, at(y * slot, slot)], "in", t)
            local(resid.at[:, c, rows(t), own_cols], rbuf.at[t, c], "in", t)
    for j in range(2):
        local(out_proj.at[:, to_cols(j, 0)], obuf.at[at(y * slot, slot), pl.ds(j * slot, slot)], "proj")
    local(enc, encv, "enc")
    local(dec, decv, "dec")

    barrier = pltpu.get_barrier_semaphore()
    greeted = [*y_at[1:], *z_at[1:], x_at, xl_at, core_at]
    for where in greeted:
        pl.semaphore_signal(barrier, inc=1, device_id=where, device_id_type=MESH)
    pl.semaphore_wait(barrier, len(greeted))

    def send_heads(t):
        for c, k, name in ((0, 1, "relay"), (1, 3, "relay"), (1, 1, "heads"), (0, 3, "heads")):
            kind = (name, k) if name == "relay" else (name,)
            send(heads.at[:, c, rows(t), :], hbuf.at[t, c, :, :, at(y * slot, slot)], y_at[k], t, *kind)

    def send_proj(t, which):
        for j in range(2):
            for k in which:
                send(
                    out_proj.at[:, to_cols(j, k)], obuf.at[at(y * slot, slot), pl.ds(j * slot, slot)], y_at[k],
                    0, "proj",
                )

    def relay_heads(t):
        for c, k, back in ((0, 1, 3), (1, 3, 1)):
            arrived(t, "relay", k)
            part = hbuf.at[t, c, :, :, at(yc[back] * slot, slot)]
            send(part, part, y_at[k], t, "heads")

    def project(t):
        if first("proj"):
            fetched("proj")
            arrived(0, "proj")
        fetched("in", t)
        arrived(t, "heads")
        value = dot(hbuf[t].reshape(token_rows, half), obuf[...])
        psend[t] = value[:, :slot].reshape(2, side, slot)
        for h in range(2):
            send(psend.at[t, h], precv.at[t, h], x_at, t, "part", h)
        pown[t] = value[:, slot:].reshape(2, side, slot)

    def ring_send(name, t, h, cols):
        for k in (1, 3):
            part = hid.at[t, pl.ds(h * side, side), cols]
            send(part, part, y_at[k], t, *((name, k) if h == (k == 3) else ("hid",)))

    def ring_relay(name, t, which_xh):
        for h, k, back in ((0, 1, 3), (1, 3, 1)):
            arrived(t, name, k)
            part = hid.at[t, pl.ds(h * side, side), at((which_xh * 4 + yc[back]) * slot, slot)]
            send(part, part, y_at[k], t, "hid")

    def hide(t, h):
        arrived(t, "part", h)
        projected = pown[t, h] + precv[t, h]
        residual = rbuf[t, h].reshape(side, slot).astype(F32)
        here = pl.ds(h * side, side)
        hid[t, here, own_cols] = (residual + projected).astype(BF16)
        part = hid.at[t, here, own_cols]
        send(part, part, x_at, t, "pair", h)
        ring_send("ring", t, h, own_cols)

    def spread_own(t):
        ring_relay("ring", t, xh)

    def spread_partner(t, h):
        arrived(t, "pair", h)
        ring_send("other", t, h, partner_cols)

    def relay_partner(t):
        ring_relay("other", t, 1 - xh)

    width = feats // PIECES
    tile_width = width // PARTS

    def encode(t, q):
        if first("enc"):
            fetched("enc")
        if q == 0:
            arrived(t, "hid")
        cols = pl.ds(q * width, width)
        ebuf[t, :, cols] = dot(hid[t], encv[:, cols])
        for part in range(PARTS):
            cols = pl.ds(q * width + part * tile_width, tile_width)
            send(ebuf.at[t, at((1 - core) * side, side), cols], erecv.at[t, :, cols], core_at, t, "core", q)

    def sum_core(t, q):
        cols = pl.ds(q * width, width)
        arrived(t, "core", q)
        for k in (2, 1, 3, 0):
            total = ebuf[t, block(zc[k]), cols] + erecv[t, at(zc[k] * 2 * ROWS, 2 * ROWS), cols]
            if k:
                zsend[t, k - 1, :, cols] = total.astype(BF16)
                send(zsend.at[t, k - 1, :, cols], zrecv.at[t, k - 1, :, cols], z_at[k], t, "zsum", q)
            else:
                ebuf[t, block(z), cols] = total

    def sum_near(t, q):
        cols = pl.ds(q * width, width)
        arrived(t, "zsum", q)
        total = ebuf[t, block(z), cols]
        for k in range(3):
            total = total + zrecv[t, k, :, cols].astype(F32)
        ztot[t, :, cols] = total
        send(ztot.at[t, :, cols], xlrecv.at[t, :, cols], xl_at, t, "xl", q)

    def activate(t, q):
        cols = pl.ds(q * width, width)
        arrived(t, "xl", q)
        active = jnp.maximum(ztot[t, :, cols] + xlrecv[t, :, cols] + enc_bias[:, cols], 0.0)
        here = block(z)
        coded[t, here, cols] = active.astype(BF16)
        part = coded.at[t, here, cols]
        for k in (2, 1, 3):
            send(part, part, z_at[k], t, "code", q, k)
        send(part, part, core_at, t, "coded")
        fout[t, :, cols] = active
        local(fout.at[t, at(xl * ROWS, ROWS), cols], features.at[rows(t), cols], "out")

    def gather_core(t, q):
        for k in (1, 3, 2):
            arrived(t, "code", q, k)
            part = coded.at[t, block(zc[4 - k]), pl.ds(q * width, width)]
            send(part, part, core_at, t, "coded")

    def decode(t):
        if first("dec"):
            fetched("dec")
        arrived(t, "coded")
        low, high = pl.ds(0, side), pl.ds(side, side)
        for j in range(2):
            cols = at((xh if j else 1 - xh) * half, half)
            acc[t, :, cols] = dot(coded[t], decv[:, cols])
            s1[t, j] = acc[t, :, to_cols(j, 2)].astype(BF16).reshape(2, side, slot)
            s2[t, j, 0, 1] = acc[t, high, to_cols(j, 1)].astype(BF16)
            s2[t, j, 1, 0] = acc[t, low, to_cols(j, 3)].astype(BF16)
            send(s1.at[t, j, 0], r1.at[t, j, 0], y_at[1], t, "far", j, 0)
            send(s1.at[t, j, 1], r1.at[t, j, 1], y_at[3], t, "far", j, 1)
            send(s2.at[t, j, 0, 1], r2.at[t, j, 0, 1], y_at[1], t, "near", j)
            send(s2.at[t, j, 1, 0], r2.at[t, j, 1, 0], y_at[3], t, "near", j)

    def sum_relay(t, j):
        for d, k, h in ((0, 1, pl.ds(0, side)), (1, 3, pl.ds(side, side))):
            arrived(t, "far", j, d)
            s2[t, j, d, d] = (acc[t, h, to_cols(j, k)] + r1[t, j, d].astype(F32)).astype(BF16)
            send(s2.at[t, j, d, d], r2.at[t, j, d, d], y_at[k], t, "near", j)

    def last_pair(t):
        return (s4, r4) if t == chunks - 1 else (s3.at[t], r3.at[t])

    def sum_ring(t, j):
        arrived(t, "near", j)
        cols = to_cols(j, 0)
        src, dst = last_pair(t)
        for h in range(2):
            here = pl.ds(h * side, side)
            total = acc[t, here, cols] + r2[t, j, 0, h].astype(F32) + r2[t, j, 1, h].astype(F32)
            if j == 1:
                acc[t, here, cols] = total
            else:
                src[h] = total.astype(src.dtype)
        if j == 0:
            send(src, dst, x_at, t, "last")

    def finish(t):
        arrived(t, "last")
        cols = to_cols(1, 0)
        other = last_pair(t)[1]
        for h in range(2):
            total = acc[t, pl.ds(h * side, side), cols] + other[h].astype(F32) + dec_bias[...]
            rout[t, h] = total.reshape(8, ROWS, slot)
            local(rout.at[t, h], rebuilt.at[:, h, rows(t), :], "out")

    def each(step, count):
        return [functools.partial(lambda t, n: step(t, n), n=n) for n in range(count)]

    steps = [
        send_heads, lambda t: send_proj(t, (2,)), lambda t: send_proj(t, (1, 3)), relay_heads, project, *each(hide, 2),
        spread_own, *each(spread_partner, 2), relay_partner, *each(encode, PIECES), *each(sum_core, PIECES),
        *each(sum_near, PIECES), *each(activate, PIECES), *each(gather_core, PIECES),
        decode, *each(sum_relay, 2), *each(sum_ring, 2), finish,
    ]
    for step, t in ORDER:
        steps[step](t)
    fetched("out")
    for t in range(chunks):
        settle(sent, send_sem, t)


def per_device(attn_heads, out_proj, resid_pre, enc_weight, enc_bias, dec_weight, dec_bias):
    _, tokens, slot = attn_heads.shape
    width = resid_pre.shape[2]
    feats = enc_weight.shape[2]
    per_owner = tokens // LAYERS
    chunks = per_owner // ROWS
    side = LAYERS * ROWS // 2
    two = 2 * slot
    vmem, anywhere = pl.BlockSpec(memory_space=pltpu.VMEM), pl.BlockSpec(memory_space=pl.ANY)
    features, rebuilt = pl.pallas_call(
        functools.partial(kernel, chunks),
        out_shape=(
            jax.ShapeDtypeStruct((per_owner, feats), F32),
            jax.ShapeDtypeStruct((8, 2, per_owner, slot), F32),
        ),
        in_specs=[anywhere, anywhere, anywhere, anywhere, vmem, anywhere, vmem],
        out_specs=(anywhere, anywhere),
        scratch_shapes=[
            pltpu.VMEM((chunks, 2, 8, ROWS, 4 * slot), BF16),
            pltpu.VMEM((4 * slot, two), BF16),
            pltpu.VMEM((chunks, 2, 8, ROWS, slot), BF16),
            pltpu.VMEM((chunks, 2, side, slot), F32),
            pltpu.VMEM((chunks, 2, side, slot), F32),
            pltpu.VMEM((chunks, 2, side, slot), F32),
            pltpu.VMEM((chunks, 2 * side, width), BF16),
            pltpu.VMEM((width, feats), BF16),
            pltpu.VMEM((feats, width), BF16),
            pltpu.VMEM((chunks, 2 * side, feats), F32),
            pltpu.VMEM((chunks, side, feats), F32),
            pltpu.VMEM((chunks, 3, 2 * ROWS, feats), BF16),
            pltpu.VMEM((chunks, 3, 2 * ROWS, feats), BF16),
            pltpu.VMEM((chunks, 2 * ROWS, feats), F32),
            pltpu.VMEM((chunks, 2 * ROWS, feats), F32),
            pltpu.VMEM((chunks, 2 * side, feats), BF16),
            pltpu.VMEM((chunks, 2 * side, width), F32),
            pltpu.VMEM((chunks, 2, 2, side, slot), BF16),
            pltpu.VMEM((chunks, 2, 2, side, slot), BF16),
            pltpu.VMEM((chunks, 2, 2, 2, side, slot), BF16),
            pltpu.VMEM((chunks, 2, 2, 2, side, slot), BF16),
            pltpu.VMEM((chunks - 1, 2, side, slot), F32),
            pltpu.VMEM((chunks - 1, 2, side, slot), F32),
            pltpu.VMEM((2, side, slot), BF16),
            pltpu.VMEM((2, side, slot), BF16),
            pltpu.VMEM((chunks, 2 * ROWS, feats), F32),
            pltpu.VMEM((chunks, 2, 8, ROWS, slot), F32),
            pltpu.SemaphoreType.DMA((chunks,)),
            pltpu.SemaphoreType.DMA((ARRIVALS,)),
            pltpu.SemaphoreType.DMA((FETCHES,)),
        ],
        compiler_params=pltpu.CompilerParams(
            collective_id=0, has_side_effects=True, vmem_limit_bytes=66_000_000
        ),
        name="crosscoder",
    )(
        attn_heads.reshape(8, 2, per_owner, slot),
        out_proj[0],
        resid_pre.reshape(8, 2, per_owner, width),
        enc_weight[0],
        enc_bias.reshape(1, feats),
        dec_weight[0],
        dec_bias,
    )
    return features, rebuilt.reshape(1, tokens, slot)


def solution(mesh):
    return jax.shard_map(
        per_device,
        mesh=mesh,
        in_specs=(
            P("layer", None, "feat"),
            P("layer", "feat", None),
            P("layer", None, None),
            P("layer", None, "feat"),
            P("feat"),
            P("layer", "feat", None),
            P("layer", "feat"),
        ),
        out_specs=(P("layer", "feat"), P("layer", None, "feat")),
        check_vma=False,
    )
```

```python
import functools
import math

import jax
import jax.numpy as jnp
from jax import lax
from jax.experimental import pallas as pl
from jax.experimental.pallas import tpu as pltpu
from jax.sharding import PartitionSpec as P

MESH = pl.DeviceIdType.MESH
LAYERS, FEATS = 16, 8
ROWS = 16
ARRIVALS, FETCHES = 97, 7
F32, BF16 = jnp.float32, jnp.bfloat16

ORDER = (
    (0, 0), (1, 0), (3, 0), (2, 0), (0, 2), (4, 0), (0, 1), (3, 1), (3, 2), (5, 0), (6, 0), (4, 1), (8, 0), (9, 0),
    (7, 0), (10, 0), (5, 1), (6, 1), (4, 2), (11, 0), (8, 1), (12, 0), (9, 1), (7, 1), (13, 0), (5, 2), (10, 1),
    (6, 2), (14, 0), (15, 0), (8, 2), (11, 1), (9, 2), (12, 1), (16, 0), (7, 2), (17, 0), (13, 1), (10, 2), (18, 0),
    (14, 1), (19, 0), (11, 2), (12, 2), (15, 1), (20, 0), (13, 2), (16, 1), (14, 2), (17, 1), (22, 0), (21, 0),
    (15, 2), (18, 1), (23, 0), (16, 2), (19, 1), (20, 1), (17, 2), (24, 0), (21, 1), (22, 1), (25, 0), (18, 2),
    (23, 1), (26, 0), (21, 2), (22, 2), (24, 1), (23, 2), (26, 1), (27, 0), (28, 0), (24, 2), (25, 1), (25, 2),
    (26, 2), (27, 1), (28, 1), (27, 2), (28, 2),
)
PIECES, PARTS = 2, 2
RELAYED = (0, 1)


def dot(a, b):
    return jnp.dot(a, b, preferred_element_type=F32)


def at(start, size):
    return pl.ds(pl.multiple_of(start, size), size)


def kernel(
    chunks, heads, out_proj, resid, enc, enc_bias, dec, dec_bias, features, rebuilt,
    hbuf, obuf, rbuf, psend, precv, pown, hid, encv, decv, ebuf, erecv, zsend, zrecv, ztot, xlrecv, coded,
    acc, s1, r1, s2, r2, s3, r3, s4, r4, fout, rout, send_sem, recv_sem, local_sem,
):
    layer, feat = lax.axis_index("layer"), lax.axis_index("feat")
    z, xl, core = layer // 4, lax.rem(layer // 2, 2), lax.rem(layer, 2)
    xh, y = feat // 4, lax.rem(feat, 4)
    yc = [lax.rem(y + k, 4) for k in range(4)]
    zc = [lax.rem(z + k, 4) for k in range(4)]
    y_at = [{"feat": xh * 4 + yc[k]} for k in range(4)]
    z_at = [{"layer": zc[k] * 4 + xl * 2 + core} for k in range(4)]
    x_at = {"feat": (1 - xh) * 4 + y}
    xl_at = {"layer": z * 4 + (1 - xl) * 2 + core}
    core_at = {"layer": z * 4 + xl * 2 + 1 - core}
    slot = out_proj.shape[0]
    half = 4 * slot
    token_rows = LAYERS * ROWS
    side = token_rows // 2
    feats = encv.shape[1]

    done, fetching, arriving, sent = set(), {}, {}, {}

    def expect(groups, sems, key, ref):
        index, size = groups.get(key, (len(groups), 0))
        assert index < sems.shape[0]
        groups[key] = index, size + math.prod(ref.shape) * ref.dtype.itemsize
        return sems.at[index]

    def settle(groups, sems, key):
        index, size = groups[key]
        view = encv.at[pl.ds(0, size // (2 * encv.shape[1]))]
        pltpu.make_async_copy(view, view, sems.at[index]).wait()

    def local(src, dst, *key):
        pltpu.make_async_copy(src, dst, expect(fetching, local_sem, key, dst)).start()

    def fetched(*key):
        settle(fetching, local_sem, key)

    def send(src, dst, where, t, *key):
        pltpu.make_async_remote_copy(
            src, dst, expect(sent, send_sem, t, src), expect(arriving, recv_sem, (t, *key), dst),
            device_id=where, device_id_type=MESH,
        ).start()

    def arrived(*key):
        settle(arriving, recv_sem, key)

    def first(name):
        fresh = name not in done
        done.add(name)
        return fresh

    def rows(t):
        return pl.ds(t * ROWS, ROWS)

    def group(which_z, which_xl):
        return at((core * 8 + which_z * 2 + which_xl) * ROWS, ROWS)

    def block(which_z):
        return at((core * 8 + which_z * 2) * ROWS, 2 * ROWS)

    own_cols = at(feat * slot, slot)
    partner_cols = at(((1 - xh) * 4 + y) * slot, slot)

    def to_cols(j, which):
        return at((xh if j else 1 - xh) * half + yc[which] * slot, slot)

    for t in range(chunks):
        for c in range(2):
            local(heads.at[:, c, rows(t), :], hbuf.at[t, c, :, :, at(y * slot, slot)], "in", t)
            local(resid.at[:, c, rows(t), own_cols], rbuf.at[t, c], "in", t)
    for j in range(2):
        local(out_proj.at[:, to_cols(j, 0)], obuf.at[at(y * slot, slot), pl.ds(j * slot, slot)], "proj")
    local(enc, encv, "enc")
    local(dec, decv, "dec")

    barrier = pltpu.get_barrier_semaphore()
    greeted = [*y_at[1:], *z_at[1:], x_at, xl_at, core_at]
    for where in greeted:
        pl.semaphore_signal(barrier, inc=1, device_id=where, device_id_type=MESH)
    pl.semaphore_wait(barrier, len(greeted))

    def send_heads(t):
        for c, k, name in ((0, 1, "relay"), (1, 3, "relay"), (1, 1, "heads"), (0, 3, "heads")):
            kind = (name, k) if name == "relay" else (name,)
            send(heads.at[:, c, rows(t), :], hbuf.at[t, c, :, :, at(y * slot, slot)], y_at[k], t, *kind)

    def send_proj(t, which):
        for j in range(2):
            for k in which:
                send(
                    out_proj.at[:, to_cols(j, k)], obuf.at[at(y * slot, slot), pl.ds(j * slot, slot)], y_at[k],
                    0, "proj",
                )

    def relay_heads(t):
        for c, k, back in ((0, 1, 3), (1, 3, 1)):
            arrived(t, "relay", k)
            part = hbuf.at[t, c, :, :, at(yc[back] * slot, slot)]
            send(part, part, y_at[k], t, "heads")

    def project(t):
        if first("proj"):
            fetched("proj")
            arrived(0, "proj")
        fetched("in", t)
        arrived(t, "heads")
        value = dot(hbuf[t].reshape(token_rows, half), obuf[...])
        psend[t] = value[:, :slot].reshape(2, side, slot)
        for h in range(2):
            send(psend.at[t, h], precv.at[t, h], x_at, t, "part", h)
        pown[t] = value[:, slot:].reshape(2, side, slot)

    def ring_send(name, t, h, cols):
        for k in (1, 3):
            part = hid.at[t, pl.ds(h * side, side), cols]
            send(part, part, y_at[k], t, *((name, k) if h == (k == 3) else ("hid",)))

    def ring_relay(name, t, which_xh):
        for h, k, back in ((0, 1, 3), (1, 3, 1)):
            arrived(t, name, k)
            part = hid.at[t, pl.ds(h * side, side), at((which_xh * 4 + yc[back]) * slot, slot)]
            send(part, part, y_at[k], t, "hid")

    def hide(t, h):
        arrived(t, "part", h)
        projected = pown[t, h] + precv[t, h]
        residual = rbuf[t, h].reshape(side, slot).astype(F32)
        here = pl.ds(h * side, side)
        hid[t, here, own_cols] = (residual + projected).astype(BF16)
        part = hid.at[t, here, own_cols]
        send(part, part, x_at, t, "pair", h)
        ring_send("ring", t, h, own_cols)

    def spread_own(t):
        ring_relay("ring", t, xh)

    def spread_partner(t, h):
        arrived(t, "pair", h)
        ring_send("other", t, h, partner_cols)

    def relay_partner(t):
        ring_relay("other", t, 1 - xh)

    width = feats // PIECES
    tile_width = width // PARTS

    def encode(t, q):
        if first("enc"):
            fetched("enc")
        if q == 0:
            arrived(t, "hid")
        cols = pl.ds(q * width, width)
        ebuf[t, :, cols] = dot(hid[t], encv[:, cols])
        for part in range(PARTS):
            cols = pl.ds(q * width + part * tile_width, tile_width)
            send(ebuf.at[t, at((1 - core) * side, side), cols], erecv.at[t, :, cols], core_at, t, "core", q)

    def sum_core(t, q):
        cols = pl.ds(q * width, width)
        arrived(t, "core", q)
        for k in (2, 1, 3, 0):
            total = ebuf[t, block(zc[k]), cols] + erecv[t, at(zc[k] * 2 * ROWS, 2 * ROWS), cols]
            if k:
                zsend[t, k - 1, :, cols] = total.astype(BF16)
                send(zsend.at[t, k - 1, :, cols], zrecv.at[t, k - 1, :, cols], z_at[k], t, "zsum", q)
            else:
                ebuf[t, block(z), cols] = total

    def sum_near(t, q):
        cols = pl.ds(q * width, width)
        arrived(t, "zsum", q)
        total = ebuf[t, block(z), cols]
        for k in range(3):
            total = total + zrecv[t, k, :, cols].astype(F32)
        ztot[t, :, cols] = total
        send(ztot.at[t, :, cols], xlrecv.at[t, :, cols], xl_at, t, "xl", q)

    def activate(t, q):
        cols = pl.ds(q * width, width)
        arrived(t, "xl", q)
        active = jnp.maximum(ztot[t, :, cols] + xlrecv[t, :, cols] + enc_bias[:, cols], 0.0)
        here = block(z)
        coded[t, here, cols] = active.astype(BF16)
        part = coded.at[t, here, cols]
        for k in (1, 3) if t in RELAYED else (2, 1, 3):
            send(part, part, z_at[k], t, "code", q, k)
        send(part, part, core_at, t, "coded")
        fout[t, :, cols] = active
        local(fout.at[t, at(xl * ROWS, ROWS), cols], features.at[rows(t), cols], "out")

    def gather_far(t, q):
        cols = pl.ds(q * width, width)
        for d, k in enumerate((1, 3)):
            arrived(t, "code", q, k)
            part = coded.at[t, group(zc[4 - k], d), cols]
            send(part, part, z_at[k], t, "code", q, 2)
            part = coded.at[t, block(zc[4 - k]), cols]
            send(part, part, core_at, t, "coded")

    def gather_core(t, q):
        for k in (2,) if t in RELAYED else (1, 3, 2):
            arrived(t, "code", q, k)
            part = coded.at[t, block(zc[4 - k]), pl.ds(q * width, width)]
            send(part, part, core_at, t, "coded")

    def decode(t):
        if first("dec"):
            fetched("dec")
        arrived(t, "coded")
        low, high = pl.ds(0, side), pl.ds(side, side)
        for j in range(2):
            cols = at((xh if j else 1 - xh) * half, half)
            acc[t, :, cols] = dot(coded[t], decv[:, cols])
            s1[t, j] = acc[t, :, to_cols(j, 2)].astype(BF16).reshape(2, side, slot)
            s2[t, j, 0, 1] = acc[t, high, to_cols(j, 1)].astype(BF16)
            s2[t, j, 1, 0] = acc[t, low, to_cols(j, 3)].astype(BF16)
            send(s1.at[t, j, 0], r1.at[t, j, 0], y_at[1], t, "far", j, 0)
            send(s1.at[t, j, 1], r1.at[t, j, 1], y_at[3], t, "far", j, 1)
            send(s2.at[t, j, 0, 1], r2.at[t, j, 0, 1], y_at[1], t, "near", j)
            send(s2.at[t, j, 1, 0], r2.at[t, j, 1, 0], y_at[3], t, "near", j)

    def sum_relay(t, j):
        for d, k, h in ((0, 1, pl.ds(0, side)), (1, 3, pl.ds(side, side))):
            arrived(t, "far", j, d)
            s2[t, j, d, d] = (acc[t, h, to_cols(j, k)] + r1[t, j, d].astype(F32)).astype(BF16)
            send(s2.at[t, j, d, d], r2.at[t, j, d, d], y_at[k], t, "near", j)

    def last_pair(t):
        return (s4, r4) if t == chunks - 1 else (s3.at[t], r3.at[t])

    def sum_ring(t, j):
        arrived(t, "near", j)
        cols = to_cols(j, 0)
        src, dst = last_pair(t)
        for h in range(2):
            here = pl.ds(h * side, side)
            total = acc[t, here, cols] + r2[t, j, 0, h].astype(F32) + r2[t, j, 1, h].astype(F32)
            if j == 1:
                acc[t, here, cols] = total
            else:
                src[h] = total.astype(src.dtype)
        if j == 0:
            send(src, dst, x_at, t, "last")

    def finish(t):
        arrived(t, "last")
        cols = to_cols(1, 0)
        other = last_pair(t)[1]
        for h in range(2):
            total = acc[t, pl.ds(h * side, side), cols] + other[h].astype(F32) + dec_bias[...]
            rout[t, h] = total.reshape(8, ROWS, slot)
            local(rout.at[t, h], rebuilt.at[:, h, rows(t), :], "out")

    def each(step, count):
        return [functools.partial(lambda t, n: step(t, n), n=n) for n in range(count)]

    steps = [
        send_heads, lambda t: send_proj(t, (2,)), lambda t: send_proj(t, (1, 3)), relay_heads, project, *each(hide, 2),
        spread_own, *each(spread_partner, 2), relay_partner, *each(encode, PIECES), *each(sum_core, PIECES),
        *each(sum_near, PIECES), *each(activate, PIECES), *each(gather_far, PIECES), *each(gather_core, PIECES),
        decode, *each(sum_relay, 2), *each(sum_ring, 2), finish,
    ]
    for step, t in ORDER:
        steps[step](t)
    fetched("out")
    for t in range(chunks):
        settle(sent, send_sem, t)


def hand_on(features, rebuilt, features_out, rebuilt_out, first, second, came_in, went_out):
    parts = [(features, first, features_out)]
    parts += [(rebuilt.at[rows], second.at[rows], rebuilt_out.at[rows]) for rows in (pl.ds(0, 4), pl.ds(4, 4))]
    moves_in = [pltpu.make_async_copy(a, b, came_in.at[i]) for i, (a, b, _) in enumerate(parts)]
    moves_out = [pltpu.make_async_copy(b, c, went_out.at[i]) for i, (_, b, c) in enumerate(parts)]
    for move in moves_in:
        move.start()
    for move_in, move_out in zip(moves_in, moves_out):
        move_in.wait()
        move_out.start()
    for move in moves_out:
        move.wait()


def per_device(attn_heads, out_proj, resid_pre, enc_weight, enc_bias, dec_weight, dec_bias):
    _, tokens, slot = attn_heads.shape
    width = resid_pre.shape[2]
    feats = enc_weight.shape[2]
    per_owner = tokens // LAYERS
    chunks = per_owner // ROWS
    side = LAYERS * ROWS // 2
    two = 2 * slot
    vmem, anywhere = pl.BlockSpec(memory_space=pltpu.VMEM), pl.BlockSpec(memory_space=pl.ANY)
    shapes = (
        jax.ShapeDtypeStruct((per_owner, feats), F32),
        jax.ShapeDtypeStruct((8, 2, per_owner, slot), F32),
    )
    results = pl.pallas_call(
        functools.partial(kernel, chunks),
        out_shape=shapes,
        in_specs=[anywhere, anywhere, anywhere, anywhere, vmem, anywhere, vmem],
        out_specs=(anywhere, anywhere),
        scratch_shapes=[
            pltpu.VMEM((chunks, 2, 8, ROWS, 4 * slot), BF16),
            pltpu.VMEM((4 * slot, two), BF16),
            pltpu.VMEM((chunks, 2, 8, ROWS, slot), BF16),
            pltpu.VMEM((chunks, 2, side, slot), F32),
            pltpu.VMEM((chunks, 2, side, slot), F32),
            pltpu.VMEM((chunks, 2, side, slot), F32),
            pltpu.VMEM((chunks, 2 * side, width), BF16),
            pltpu.VMEM((width, feats), BF16),
            pltpu.VMEM((feats, width), BF16),
            pltpu.VMEM((chunks, 2 * side, feats), F32),
            pltpu.VMEM((chunks, side, feats), F32),
            pltpu.VMEM((chunks, 3, 2 * ROWS, feats), BF16),
            pltpu.VMEM((chunks, 3, 2 * ROWS, feats), BF16),
            pltpu.VMEM((chunks, 2 * ROWS, feats), F32),
            pltpu.VMEM((chunks, 2 * ROWS, feats), F32),
            pltpu.VMEM((chunks, 2 * side, feats), BF16),
            pltpu.VMEM((chunks, 2 * side, width), F32),
            pltpu.VMEM((chunks, 2, 2, side, slot), BF16),
            pltpu.VMEM((chunks, 2, 2, side, slot), BF16),
            pltpu.VMEM((chunks, 2, 2, 2, side, slot), BF16),
            pltpu.VMEM((chunks, 2, 2, 2, side, slot), BF16),
            pltpu.VMEM((chunks - 1, 2, side, slot), F32),
            pltpu.VMEM((chunks - 1, 2, side, slot), F32),
            pltpu.VMEM((2, side, slot), BF16),
            pltpu.VMEM((2, side, slot), BF16),
            pltpu.VMEM((chunks, 2 * ROWS, feats), F32),
            pltpu.VMEM((chunks, 2, 8, ROWS, slot), F32),
            pltpu.SemaphoreType.DMA((chunks,)),
            pltpu.SemaphoreType.DMA((ARRIVALS,)),
            pltpu.SemaphoreType.DMA((FETCHES,)),
        ],
        compiler_params=pltpu.CompilerParams(
            collective_id=0, has_side_effects=True, vmem_limit_bytes=66_000_000
        ),
        name="crosscoder",
    )(
        attn_heads.reshape(8, 2, per_owner, slot),
        out_proj[0],
        resid_pre.reshape(8, 2, per_owner, width),
        enc_weight[0],
        enc_bias.reshape(1, feats),
        dec_weight[0],
        dec_bias,
    )
    features, rebuilt = pl.pallas_call(
        hand_on,
        out_shape=shapes,
        in_specs=[anywhere, anywhere],
        out_specs=(anywhere, anywhere),
        scratch_shapes=[
            *(pltpu.VMEM(shape.shape, shape.dtype) for shape in shapes),
            pltpu.SemaphoreType.DMA((3,)),
            pltpu.SemaphoreType.DMA((3,)),
        ],
        name="hand_on",
    )(*results)
    return features, rebuilt.reshape(1, tokens, slot)


def solution(mesh):
    return jax.shard_map(
        per_device,
        mesh=mesh,
        in_specs=(
            P("layer", None, "feat"),
            P("layer", "feat", None),
            P("layer", None, None),
            P("layer", None, "feat"),
            P("feat"),
            P("layer", "feat", None),
            P("layer", "feat"),
        ),
        out_specs=(P("layer", "feat"), P("layer", None, "feat")),
        check_vma=False,
    )
```

```python
import functools
import math

import jax
import jax.numpy as jnp
from jax import lax
from jax.experimental import pallas as pl
from jax.experimental.pallas import tpu as pltpu
from jax.sharding import PartitionSpec as P

MESH = pl.DeviceIdType.MESH
LAYERS, FEATS = 16, 8
ROWS = 16
ARRIVALS, FETCHES = 97, 7
F32, BF16 = jnp.float32, jnp.bfloat16

ORDER = (
    (1, 0), (0, 0), (2, 0), (3, 0), (0, 1), (4, 0), (0, 2), (3, 1), (5, 0), (3, 2), (6, 0), (4, 1), (8, 0), (9, 0),
    (7, 0), (10, 0), (5, 1), (6, 1), (4, 2), (11, 0), (8, 1), (12, 0), (9, 1), (7, 1), (13, 0), (5, 2), (10, 1),
    (6, 2), (14, 0), (15, 0), (8, 2), (11, 1), (9, 2), (12, 1), (7, 2), (16, 0), (17, 0), (10, 2), (13, 1), (18, 0),
    (14, 1), (11, 2), (12, 2), (15, 1), (20, 0), (19, 0), (13, 2), (16, 1), (14, 2), (22, 0), (21, 0), (17, 1),
    (15, 2), (18, 1), (23, 0), (16, 2), (19, 1), (20, 1), (24, 0), (17, 2), (21, 1), (22, 1), (25, 0), (18, 2),
    (23, 1), (26, 0), (21, 2), (22, 2), (24, 1), (27, 0), (23, 2), (26, 1), (28, 0), (24, 2), (25, 1), (25, 2),
    (26, 2), (27, 1), (28, 1), (27, 2), (28, 2),
)
PIECES, PARTS = 2, 2
RELAYED = (0, 1)


def dot(a, b):
    return jnp.dot(a, b, preferred_element_type=F32)


def at(start, size):
    return pl.ds(pl.multiple_of(start, size), size)


def kernel(
    chunks, heads, out_proj, resid, enc, enc_bias, dec, dec_bias, features, rebuilt,
    hbuf, obuf, rbuf, p0, q0, psend, precv, pown, hid, encv, decv, ebuf, erecv, zsend, zrecv, ztot, xlrecv, coded,
    acc, s1, r1, s2, r2, s3, r3, s4, r4, fout, rout, send_sem, recv_sem, local_sem,
):
    layer, feat = lax.axis_index("layer"), lax.axis_index("feat")
    z, xl, core = layer // 4, lax.rem(layer // 2, 2), lax.rem(layer, 2)
    xh, y = feat // 4, lax.rem(feat, 4)
    yc = [lax.rem(y + k, 4) for k in range(4)]
    zc = [lax.rem(z + k, 4) for k in range(4)]
    y_at = [{"feat": xh * 4 + yc[k]} for k in range(4)]
    z_at = [{"layer": zc[k] * 4 + xl * 2 + core} for k in range(4)]
    x_at = {"feat": (1 - xh) * 4 + y}
    xl_at = {"layer": z * 4 + (1 - xl) * 2 + core}
    core_at = {"layer": z * 4 + xl * 2 + 1 - core}
    slot = out_proj.shape[0]
    half = 4 * slot
    token_rows = LAYERS * ROWS
    side = token_rows // 2
    feats = encv.shape[1]

    done, fetching, arriving, sent = set(), {}, {}, {}

    def expect(groups, sems, key, ref):
        index, size = groups.get(key, (len(groups), 0))
        assert index < sems.shape[0]
        groups[key] = index, size + math.prod(ref.shape) * ref.dtype.itemsize
        return sems.at[index]

    def settle(groups, sems, key):
        index, size = groups[key]
        view = encv.at[pl.ds(0, size // (2 * encv.shape[1]))]
        pltpu.make_async_copy(view, view, sems.at[index]).wait()

    def local(src, dst, *key):
        pltpu.make_async_copy(src, dst, expect(fetching, local_sem, key, dst)).start()

    def fetched(*key):
        settle(fetching, local_sem, key)

    def send(src, dst, where, t, *key):
        pltpu.make_async_remote_copy(
            src, dst, expect(sent, send_sem, t, src), expect(arriving, recv_sem, (t, *key), dst),
            device_id=where, device_id_type=MESH,
        ).start()

    def arrived(*key):
        settle(arriving, recv_sem, key)

    def first(name):
        fresh = name not in done
        done.add(name)
        return fresh

    def rows(t):
        return pl.ds(t * ROWS, ROWS)

    def group(which_z, which_xl):
        return at((core * 8 + which_z * 2 + which_xl) * ROWS, ROWS)

    def block(which_z):
        return at((core * 8 + which_z * 2) * ROWS, 2 * ROWS)

    own_cols = at(feat * slot, slot)
    partner_cols = at(((1 - xh) * 4 + y) * slot, slot)

    def to_cols(j, which):
        return at((xh if j else 1 - xh) * half + yc[which] * slot, slot)

    for t in range(chunks):
        for c in range(2):
            local(heads.at[:, c, rows(t), :], hbuf.at[t, c, :, :, at(y * slot, slot)], "in", t)
            local(resid.at[:, c, rows(t), own_cols], rbuf.at[t, c], "in", t)
    for j in range(2):
        local(out_proj.at[:, to_cols(j, 0)], obuf.at[at(y * slot, slot), pl.ds(j * slot, slot)], "proj")
    local(enc, encv, "enc")
    local(dec, decv, "dec")

    barrier = pltpu.get_barrier_semaphore()
    greeted = [*y_at[1:], *z_at[1:], x_at, xl_at, core_at]
    for where in greeted:
        pl.semaphore_signal(barrier, inc=1, device_id=where, device_id_type=MESH)
    pl.semaphore_wait(barrier, len(greeted))

    def send_heads(t):
        for c, k, name in ((0, 1, "relay"), (1, 3, "relay"), (1, 1, "heads"), (0, 3, "heads")):
            kind = (name, k) if name == "relay" else (name,)
            send(heads.at[:, c, rows(t), :], hbuf.at[t, c, :, :, at(y * slot, slot)], y_at[k], t, *kind)

    def send_proj(t, which):
        for j in range(2):
            for k in which:
                send(
                    out_proj.at[:, to_cols(j, k)], obuf.at[at(y * slot, slot), pl.ds(j * slot, slot)], y_at[k],
                    0, "proj",
                )

    def relay_heads(t):
        for c, k, back in ((0, 1, 3), (1, 3, 1)):
            arrived(t, "relay", k)
            part = hbuf.at[t, c, :, :, at(yc[back] * slot, slot)]
            send(part, part, y_at[k], t, "heads")

    def first_pair(t):
        return (p0, q0) if t == 0 else (psend.at[t - 1], precv.at[t - 1])

    def project(t):
        if first("proj"):
            fetched("proj")
            arrived(0, "proj")
        fetched("in", t)
        arrived(t, "heads")
        value = dot(hbuf[t].reshape(token_rows, half), obuf[...])
        src, dst = first_pair(t)
        src[...] = value[:, :slot].reshape(2, side, slot).astype(src.dtype)
        for h in range(2):
            send(src.at[h], dst.at[h], x_at, t, "part", h)
        pown[t] = value[:, slot:].reshape(2, side, slot)

    def ring_send(name, t, h, cols):
        for k in (1, 3):
            part = hid.at[t, pl.ds(h * side, side), cols]
            send(part, part, y_at[k], t, *((name, k) if h == (k == 3) else ("hid",)))

    def ring_relay(name, t, which_xh):
        for h, k, back in ((0, 1, 3), (1, 3, 1)):
            arrived(t, name, k)
            part = hid.at[t, pl.ds(h * side, side), at((which_xh * 4 + yc[back]) * slot, slot)]
            send(part, part, y_at[k], t, "hid")

    def hide(t, h):
        arrived(t, "part", h)
        projected = pown[t, h] + first_pair(t)[1][h].astype(F32)
        residual = rbuf[t, h].reshape(side, slot).astype(F32)
        here = pl.ds(h * side, side)
        hid[t, here, own_cols] = (residual + projected).astype(BF16)
        part = hid.at[t, here, own_cols]
        send(part, part, x_at, t, "pair", h)
        ring_send("ring", t, h, own_cols)

    def spread_own(t):
        ring_relay("ring", t, xh)

    def spread_partner(t, h):
        arrived(t, "pair", h)
        ring_send("other", t, h, partner_cols)

    def relay_partner(t):
        ring_relay("other", t, 1 - xh)

    width = feats // PIECES
    tile_width = width // PARTS

    def encode(t, q):
        if first("enc"):
            fetched("enc")
        if q == 0:
            arrived(t, "hid")
        cols = pl.ds(q * width, width)
        ebuf[t, :, cols] = dot(hid[t], encv[:, cols])
        for part in range(PARTS):
            cols = pl.ds(q * width + part * tile_width, tile_width)
            send(ebuf.at[t, at((1 - core) * side, side), cols], erecv.at[t, :, cols], core_at, t, "core", q)

    def sum_core(t, q):
        cols = pl.ds(q * width, width)
        arrived(t, "core", q)
        for k in (2, 1, 3, 0):
            total = ebuf[t, block(zc[k]), cols] + erecv[t, at(zc[k] * 2 * ROWS, 2 * ROWS), cols]
            if k:
                zsend[t, k - 1, :, cols] = total.astype(BF16)
                send(zsend.at[t, k - 1, :, cols], zrecv.at[t, k - 1, :, cols], z_at[k], t, "zsum", q)
            else:
                ebuf[t, block(z), cols] = total

    def sum_near(t, q):
        cols = pl.ds(q * width, width)
        arrived(t, "zsum", q)
        total = ebuf[t, block(z), cols]
        for k in range(3):
            total = total + zrecv[t, k, :, cols].astype(F32)
        ztot[t, :, cols] = total
        send(ztot.at[t, :, cols], xlrecv.at[t, :, cols], xl_at, t, "xl", q)

    def activate(t, q):
        cols = pl.ds(q * width, width)
        arrived(t, "xl", q)
        active = jnp.maximum(ztot[t, :, cols] + xlrecv[t, :, cols] + enc_bias[:, cols], 0.0)
        here = block(z)
        coded[t, here, cols] = active.astype(BF16)
        part = coded.at[t, here, cols]
        for k in (1, 3) if t in RELAYED else (2, 1, 3):
            send(part, part, z_at[k], t, "code", q, k)
        send(part, part, core_at, t, "coded")
        fout[t, :, cols] = active
        local(fout.at[t, at(xl * ROWS, ROWS), cols], features.at[rows(t), cols], "out")

    def gather_far(t, q):
        cols = pl.ds(q * width, width)
        for d, k in enumerate((1, 3)):
            arrived(t, "code", q, k)
            part = coded.at[t, group(zc[4 - k], d), cols]
            send(part, part, z_at[k], t, "code", q, 2)
            part = coded.at[t, block(zc[4 - k]), cols]
            send(part, part, core_at, t, "coded")

    def gather_core(t, q):
        for k in (2,) if t in RELAYED else (1, 3, 2):
            arrived(t, "code", q, k)
            part = coded.at[t, block(zc[4 - k]), pl.ds(q * width, width)]
            send(part, part, core_at, t, "coded")

    def decode(t):
        if first("dec"):
            fetched("dec")
        arrived(t, "coded")
        low, high = pl.ds(0, side), pl.ds(side, side)
        for j in range(2):
            cols = at((xh if j else 1 - xh) * half, half)
            acc[t, :, cols] = dot(coded[t], decv[:, cols])
            s1[t, j] = acc[t, :, to_cols(j, 2)].astype(BF16).reshape(2, side, slot)
            s2[t, j, 0, 1] = acc[t, high, to_cols(j, 1)].astype(BF16)
            s2[t, j, 1, 0] = acc[t, low, to_cols(j, 3)].astype(BF16)
            send(s1.at[t, j, 0], r1.at[t, j, 0], y_at[1], t, "far", j, 0)
            send(s1.at[t, j, 1], r1.at[t, j, 1], y_at[3], t, "far", j, 1)
            send(s2.at[t, j, 0, 1], r2.at[t, j, 0, 1], y_at[1], t, "near", j)
            send(s2.at[t, j, 1, 0], r2.at[t, j, 1, 0], y_at[3], t, "near", j)

    def sum_relay(t, j):
        for d, k, h in ((0, 1, pl.ds(0, side)), (1, 3, pl.ds(side, side))):
            arrived(t, "far", j, d)
            s2[t, j, d, d] = (acc[t, h, to_cols(j, k)] + r1[t, j, d].astype(F32)).astype(BF16)
            send(s2.at[t, j, d, d], r2.at[t, j, d, d], y_at[k], t, "near", j)

    def last_pair(t):
        return (s4, r4) if t == chunks - 1 else (s3.at[t], r3.at[t])

    def sum_ring(t, j):
        arrived(t, "near", j)
        cols = to_cols(j, 0)
        src, dst = last_pair(t)
        for h in range(2):
            here = pl.ds(h * side, side)
            total = acc[t, here, cols] + r2[t, j, 0, h].astype(F32) + r2[t, j, 1, h].astype(F32)
            if j == 1:
                acc[t, here, cols] = total
            else:
                src[h] = total.astype(src.dtype)
        if j == 0:
            send(src, dst, x_at, t, "last")

    def finish(t):
        arrived(t, "last")
        cols = to_cols(1, 0)
        other = last_pair(t)[1]
        for h in range(2):
            total = acc[t, pl.ds(h * side, side), cols] + other[h].astype(F32) + dec_bias[...]
            rout[t, h] = total.reshape(8, ROWS, slot)
            local(rout.at[t, h], rebuilt.at[:, h, rows(t), :], "out")

    def each(step, count):
        return [functools.partial(lambda t, n: step(t, n), n=n) for n in range(count)]

    steps = [
        send_heads, lambda t: send_proj(t, (2,)), lambda t: send_proj(t, (1, 3)), relay_heads, project, *each(hide, 2),
        spread_own, *each(spread_partner, 2), relay_partner, *each(encode, PIECES), *each(sum_core, PIECES),
        *each(sum_near, PIECES), *each(activate, PIECES), *each(gather_far, PIECES), *each(gather_core, PIECES),
        decode, *each(sum_relay, 2), *each(sum_ring, 2), finish,
    ]
    for step, t in ORDER:
        steps[step](t)
    fetched("out")
    for t in range(chunks):
        settle(sent, send_sem, t)


def hand_on(features, rebuilt, features_out, rebuilt_out, first, second, came_in, went_out):
    parts = [(features, first, features_out)]
    parts += [(rebuilt.at[rows], second.at[rows], rebuilt_out.at[rows]) for rows in (pl.ds(0, 4), pl.ds(4, 4))]
    moves_in = [pltpu.make_async_copy(a, b, came_in.at[i]) for i, (a, b, _) in enumerate(parts)]
    moves_out = [pltpu.make_async_copy(b, c, went_out.at[i]) for i, (_, b, c) in enumerate(parts)]
    for move in moves_in:
        move.start()
    for move_in, move_out in zip(moves_in, moves_out):
        move_in.wait()
        move_out.start()
    for move in moves_out:
        move.wait()


def per_device(attn_heads, out_proj, resid_pre, enc_weight, enc_bias, dec_weight, dec_bias):
    _, tokens, slot = attn_heads.shape
    width = resid_pre.shape[2]
    feats = enc_weight.shape[2]
    per_owner = tokens // LAYERS
    chunks = per_owner // ROWS
    side = LAYERS * ROWS // 2
    two = 2 * slot
    vmem, anywhere = pl.BlockSpec(memory_space=pltpu.VMEM), pl.BlockSpec(memory_space=pl.ANY)
    shapes = (
        jax.ShapeDtypeStruct((per_owner, feats), F32),
        jax.ShapeDtypeStruct((8, 2, per_owner, slot), F32),
    )
    results = pl.pallas_call(
        functools.partial(kernel, chunks),
        out_shape=shapes,
        in_specs=[anywhere, anywhere, anywhere, anywhere, vmem, anywhere, vmem],
        out_specs=(anywhere, anywhere),
        scratch_shapes=[
            pltpu.VMEM((chunks, 2, 8, ROWS, 4 * slot), BF16),
            pltpu.VMEM((4 * slot, two), BF16),
            pltpu.VMEM((chunks, 2, 8, ROWS, slot), BF16),
            pltpu.VMEM((2, side, slot), BF16),
            pltpu.VMEM((2, side, slot), BF16),
            pltpu.VMEM((chunks - 1, 2, side, slot), F32),
            pltpu.VMEM((chunks - 1, 2, side, slot), F32),
            pltpu.VMEM((chunks, 2, side, slot), F32),
            pltpu.VMEM((chunks, 2 * side, width), BF16),
            pltpu.VMEM((width, feats), BF16),
            pltpu.VMEM((feats, width), BF16),
            pltpu.VMEM((chunks, 2 * side, feats), F32),
            pltpu.VMEM((chunks, side, feats), F32),
            pltpu.VMEM((chunks, 3, 2 * ROWS, feats), BF16),
            pltpu.VMEM((chunks, 3, 2 * ROWS, feats), BF16),
            pltpu.VMEM((chunks, 2 * ROWS, feats), F32),
            pltpu.VMEM((chunks, 2 * ROWS, feats), F32),
            pltpu.VMEM((chunks, 2 * side, feats), BF16),
            pltpu.VMEM((chunks, 2 * side, width), F32),
            pltpu.VMEM((chunks, 2, 2, side, slot), BF16),
            pltpu.VMEM((chunks, 2, 2, side, slot), BF16),
            pltpu.VMEM((chunks, 2, 2, 2, side, slot), BF16),
            pltpu.VMEM((chunks, 2, 2, 2, side, slot), BF16),
            pltpu.VMEM((chunks - 1, 2, side, slot), F32),
            pltpu.VMEM((chunks - 1, 2, side, slot), F32),
            pltpu.VMEM((2, side, slot), BF16),
            pltpu.VMEM((2, side, slot), BF16),
            pltpu.VMEM((chunks, 2 * ROWS, feats), F32),
            pltpu.VMEM((chunks, 2, 8, ROWS, slot), F32),
            pltpu.SemaphoreType.DMA((chunks,)),
            pltpu.SemaphoreType.DMA((ARRIVALS,)),
            pltpu.SemaphoreType.DMA((FETCHES,)),
        ],
        compiler_params=pltpu.CompilerParams(
            collective_id=0, has_side_effects=True, vmem_limit_bytes=66_000_000
        ),
        name="crosscoder",
    )(
        attn_heads.reshape(8, 2, per_owner, slot),
        out_proj[0],
        resid_pre.reshape(8, 2, per_owner, width),
        enc_weight[0],
        enc_bias.reshape(1, feats),
        dec_weight[0],
        dec_bias,
    )
    features, rebuilt = pl.pallas_call(
        hand_on,
        out_shape=shapes,
        in_specs=[anywhere, anywhere],
        out_specs=(anywhere, anywhere),
        scratch_shapes=[
            *(pltpu.VMEM(shape.shape, shape.dtype) for shape in shapes),
            pltpu.SemaphoreType.DMA((3,)),
            pltpu.SemaphoreType.DMA((3,)),
        ],
        name="hand_on",
    )(*results)
    return features, rebuilt.reshape(1, tokens, slot)


def solution(mesh):
    return jax.shard_map(
        per_device,
        mesh=mesh,
        in_specs=(
            P("layer", None, "feat"),
            P("layer", "feat", None),
            P("layer", None, None),
            P("layer", None, "feat"),
            P("feat"),
            P("layer", "feat", None),
            P("layer", "feat"),
        ),
        out_specs=(P("layer", "feat"), P("layer", None, "feat")),
        check_vma=False,
    )
```

```python
import functools
import math

import jax
import jax.numpy as jnp
from jax import lax
from jax.experimental import pallas as pl
from jax.experimental.pallas import tpu as pltpu
from jax.sharding import PartitionSpec as P

MESH = pl.DeviceIdType.MESH
LAYERS, FEATS = 16, 8
ROWS = 16
ARRIVALS, FETCHES = 97, 7
F32, BF16 = jnp.float32, jnp.bfloat16

ORDER = (
    (0, 0), (1, 0), (2, 0), (3, 0), (0, 1), (4, 0), (0, 2), (3, 1), (5, 0), (6, 0), (3, 2), (4, 1), (8, 0), (9, 0),
    (7, 0), (5, 1), (10, 0), (6, 1), (4, 2), (8, 1), (11, 0), (9, 1), (12, 0), (7, 1), (13, 0), (10, 1), (5, 2),
    (6, 2), (14, 0), (11, 1), (8, 2), (15, 0), (9, 2), (12, 1), (16, 0), (7, 2), (13, 1), (10, 2), (17, 0), (18, 0),
    (14, 1), (11, 2), (12, 2), (15, 1), (20, 0), (19, 0), (13, 2), (16, 1), (22, 0), (21, 0), (14, 2), (17, 1),
    (15, 2), (18, 1), (23, 0), (16, 2), (19, 1), (20, 1), (17, 2), (24, 0), (21, 1), (22, 1), (18, 2), (25, 0),
    (23, 1), (21, 2), (26, 0), (22, 2), (27, 0), (24, 1), (23, 2), (26, 1), (28, 0), (24, 2), (25, 1), (26, 2),
    (25, 2), (27, 1), (28, 1), (27, 2), (28, 2),
)
PIECES, PARTS = 2, 2
RELAYED = (0, 1)


def dot(a, b):
    return jnp.dot(a, b, preferred_element_type=F32)


def at(start, size):
    return pl.ds(pl.multiple_of(start, size), size)


def kernel(
    chunks, heads, out_proj, resid, enc, enc_bias, dec, dec_bias, features, rebuilt,
    hbuf, obuf, rbuf, p0, q0, psend, precv, pown, hid, encv, decv, ebuf, erecv, zsend, zrecv, ztot, xlrecv, coded,
    acc, s1, r1, s2, r2, s3, r3, s4, r4, fout, rout, send_sem, recv_sem, local_sem,
):
    layer, feat = lax.axis_index("layer"), lax.axis_index("feat")
    z, xl, core = layer // 4, lax.rem(layer // 2, 2), lax.rem(layer, 2)
    xh, y = feat // 4, lax.rem(feat, 4)
    yc = [lax.rem(y + k, 4) for k in range(4)]
    zc = [lax.rem(z + k, 4) for k in range(4)]
    y_at = [{"feat": xh * 4 + yc[k]} for k in range(4)]
    z_at = [{"layer": zc[k] * 4 + xl * 2 + core} for k in range(4)]
    x_at = {"feat": (1 - xh) * 4 + y}
    xl_at = {"layer": z * 4 + (1 - xl) * 2 + core}
    core_at = {"layer": z * 4 + xl * 2 + 1 - core}
    slot = out_proj.shape[0]
    half = 4 * slot
    token_rows = LAYERS * ROWS
    side = token_rows // 2
    feats = encv.shape[1]

    done, fetching, arriving, sent = set(), {}, {}, {}

    def expect(groups, sems, key, ref):
        index, size = groups.get(key, (len(groups), 0))
        assert index < sems.shape[0]
        groups[key] = index, size + math.prod(ref.shape) * ref.dtype.itemsize
        return sems.at[index]

    def settle(groups, sems, key):
        index, size = groups[key]
        view = encv.at[pl.ds(0, size // (2 * encv.shape[1]))]
        pltpu.make_async_copy(view, view, sems.at[index]).wait()

    def local(src, dst, *key):
        pltpu.make_async_copy(src, dst, expect(fetching, local_sem, key, dst)).start()

    def fetched(*key):
        settle(fetching, local_sem, key)

    def send(src, dst, where, t, *key):
        pltpu.make_async_remote_copy(
            src, dst, expect(sent, send_sem, t, src), expect(arriving, recv_sem, (t, *key), dst),
            device_id=where, device_id_type=MESH,
        ).start()

    def arrived(*key):
        settle(arriving, recv_sem, key)

    def first(name):
        fresh = name not in done
        done.add(name)
        return fresh

    def rows(t):
        return pl.ds(t * ROWS, ROWS)

    def group(which_z, which_xl):
        return at((core * 8 + which_z * 2 + which_xl) * ROWS, ROWS)

    def block(which_z):
        return at((core * 8 + which_z * 2) * ROWS, 2 * ROWS)

    own_cols = at(feat * slot, slot)
    partner_cols = at(((1 - xh) * 4 + y) * slot, slot)

    def to_cols(j, which):
        return at((xh if j else 1 - xh) * half + yc[which] * slot, slot)

    for t in range(chunks):
        for c in range(2):
            local(heads.at[:, c, rows(t), :], hbuf.at[t, c, :, :, at(y * slot, slot)], "in", t)
            local(resid.at[:, c, rows(t), own_cols], rbuf.at[t, c], "in", t)
    for j in range(2):
        local(out_proj.at[:, to_cols(j, 0)], obuf.at[at(y * slot, slot), pl.ds(j * slot, slot)], "proj")
    local(enc, encv, "enc")
    local(dec, decv, "dec")

    barrier = pltpu.get_barrier_semaphore()
    greeted = [*y_at[1:], *z_at[1:], x_at, xl_at, core_at]
    for where in greeted:
        pl.semaphore_signal(barrier, inc=1, device_id=where, device_id_type=MESH)
    pl.semaphore_wait(barrier, len(greeted))

    def send_heads(t):
        for c, k, name in ((0, 1, "relay"), (1, 3, "relay"), (1, 1, "heads"), (0, 3, "heads")):
            kind = (name, k) if name == "relay" else (name,)
            send(heads.at[:, c, rows(t), :], hbuf.at[t, c, :, :, at(y * slot, slot)], y_at[k], t, *kind)

    def send_proj(t, which):
        for j in range(2):
            for k in which:
                send(
                    out_proj.at[:, to_cols(j, k)], obuf.at[at(y * slot, slot), pl.ds(j * slot, slot)], y_at[k],
                    0, "proj",
                )

    def relay_heads(t):
        for c, k, back in ((0, 1, 3), (1, 3, 1)):
            arrived(t, "relay", k)
            part = hbuf.at[t, c, :, :, at(yc[back] * slot, slot)]
            send(part, part, y_at[k], t, "heads")

    def first_pair(t):
        return (p0, q0) if t == 0 else (psend.at[t - 1], precv.at[t - 1])

    def project(t):
        if first("proj"):
            fetched("proj")
            arrived(0, "proj")
        fetched("in", t)
        arrived(t, "heads")
        value = dot(hbuf[t].reshape(token_rows, half), obuf[...])
        src, dst = first_pair(t)
        src[...] = value[:, :slot].reshape(2, side, slot).astype(src.dtype)
        for h in range(2):
            send(src.at[h], dst.at[h], x_at, t, "part", h)
        pown[t] = value[:, slot:].reshape(2, side, slot)

    def ring_send(name, t, h, cols):
        for k in (1, 3):
            part = hid.at[t, pl.ds(h * side, side), cols]
            send(part, part, y_at[k], t, *((name, k) if h == (k == 3) else ("hid",)))

    def ring_relay(name, t, which_xh):
        for h, k, back in ((0, 1, 3), (1, 3, 1)):
            arrived(t, name, k)
            part = hid.at[t, pl.ds(h * side, side), at((which_xh * 4 + yc[back]) * slot, slot)]
            send(part, part, y_at[k], t, "hid")

    def hide(t, h):
        arrived(t, "part", h)
        projected = pown[t, h] + first_pair(t)[1][h].astype(F32)
        residual = rbuf[t, h].reshape(side, slot).astype(F32)
        here = pl.ds(h * side, side)
        hid[t, here, own_cols] = (residual + projected).astype(BF16)
        part = hid.at[t, here, own_cols]
        send(part, part, x_at, t, "pair", h)
        ring_send("ring", t, h, own_cols)

    def spread_own(t):
        ring_relay("ring", t, xh)

    def spread_partner(t, h):
        arrived(t, "pair", h)
        ring_send("other", t, h, partner_cols)

    def relay_partner(t):
        ring_relay("other", t, 1 - xh)

    width = feats // PIECES
    tile_width = width // PARTS

    def encode(t, q):
        if first("enc"):
            fetched("enc")
        if q == 0:
            arrived(t, "hid")
        cols = pl.ds(q * width, width)
        ebuf[t, :, cols] = dot(hid[t], encv[:, cols])
        for part in range(PARTS):
            cols = pl.ds(q * width + part * tile_width, tile_width)
            send(ebuf.at[t, at((1 - core) * side, side), cols], erecv.at[t, :, cols], core_at, t, "core", q)

    def sum_core(t, q):
        cols = pl.ds(q * width, width)
        arrived(t, "core", q)
        for k in (2, 1, 3, 0):
            total = ebuf[t, block(zc[k]), cols] + erecv[t, at(zc[k] * 2 * ROWS, 2 * ROWS), cols]
            if k:
                zsend[t, k - 1, :, cols] = total.astype(BF16)
                send(zsend.at[t, k - 1, :, cols], zrecv.at[t, k - 1, :, cols], z_at[k], t, "zsum", q)
            else:
                ebuf[t, block(z), cols] = total

    def sum_near(t, q):
        cols = pl.ds(q * width, width)
        arrived(t, "zsum", q)
        total = ebuf[t, block(z), cols]
        for k in range(3):
            total = total + zrecv[t, k, :, cols].astype(F32)
        ztot[t, :, cols] = total
        send(ztot.at[t, :, cols], xlrecv.at[t, :, cols], xl_at, t, "xl", q)

    def activate(t, q):
        cols = pl.ds(q * width, width)
        arrived(t, "xl", q)
        active = jnp.maximum(ztot[t, :, cols] + xlrecv[t, :, cols] + enc_bias[:, cols], 0.0)
        here = block(z)
        coded[t, here, cols] = active.astype(BF16)
        part = coded.at[t, here, cols]
        for k in (1, 3) if t in RELAYED else (2, 1, 3):
            send(part, part, z_at[k], t, "code", q, k)
        send(part, part, core_at, t, "coded")
        fout[t, :, cols] = active
        local(fout.at[t, at(xl * ROWS, ROWS), cols], features.at[rows(t), cols], "out")

    def gather_far(t, q):
        cols = pl.ds(q * width, width)
        for d, k in enumerate((1, 3)):
            arrived(t, "code", q, k)
            part = coded.at[t, group(zc[4 - k], d), cols]
            send(part, part, z_at[k], t, "code", q, 2)
            part = coded.at[t, block(zc[4 - k]), cols]
            send(part, part, core_at, t, "coded")

    def gather_core(t, q):
        for k in (2,) if t in RELAYED else (1, 3, 2):
            arrived(t, "code", q, k)
            part = coded.at[t, block(zc[4 - k]), pl.ds(q * width, width)]
            send(part, part, core_at, t, "coded")

    def decode(t):
        if first("dec"):
            fetched("dec")
        arrived(t, "coded")
        low, high = pl.ds(0, side), pl.ds(side, side)
        for j in range(2):
            cols = at((xh if j else 1 - xh) * half, half)
            acc[t, :, cols] = dot(coded[t], decv[:, cols])
            s1[t, j] = acc[t, :, to_cols(j, 2)].astype(BF16).reshape(2, side, slot)
            s2[t, j, 0, 1] = acc[t, high, to_cols(j, 1)].astype(BF16)
            s2[t, j, 1, 0] = acc[t, low, to_cols(j, 3)].astype(BF16)
            send(s1.at[t, j, 0], r1.at[t, j, 0], y_at[1], t, "far", j, 0)
            send(s1.at[t, j, 1], r1.at[t, j, 1], y_at[3], t, "far", j, 1)
            send(s2.at[t, j, 0, 1], r2.at[t, j, 0, 1], y_at[1], t, "near", j)
            send(s2.at[t, j, 1, 0], r2.at[t, j, 1, 0], y_at[3], t, "near", j)

    def sum_relay(t, j):
        for d, k, h in ((0, 1, pl.ds(0, side)), (1, 3, pl.ds(side, side))):
            arrived(t, "far", j, d)
            s2[t, j, d, d] = (acc[t, h, to_cols(j, k)] + r1[t, j, d].astype(F32)).astype(BF16)
            send(s2.at[t, j, d, d], r2.at[t, j, d, d], y_at[k], t, "near", j)

    def last_pair(t):
        return (s4, r4) if t == chunks - 1 else (s3.at[t], r3.at[t])

    def sum_ring(t, j):
        arrived(t, "near", j)
        cols = to_cols(j, 0)
        src, dst = last_pair(t)
        for h in range(2):
            here = pl.ds(h * side, side)
            total = acc[t, here, cols] + r2[t, j, 0, h].astype(F32) + r2[t, j, 1, h].astype(F32)
            if j == 1:
                acc[t, here, cols] = total
            else:
                src[h] = total.astype(src.dtype)
        if j == 0:
            send(src, dst, x_at, t, "last")

    def finish(t):
        arrived(t, "last")
        cols = to_cols(1, 0)
        other = last_pair(t)[1]
        for h in range(2):
            total = acc[t, pl.ds(h * side, side), cols] + other[h].astype(F32) + dec_bias[...]
            rout[t, h] = total.reshape(8, ROWS, slot)
            local(rout.at[t, h], rebuilt.at[:, h, rows(t), :], "out")

    def each(step, count):
        return [functools.partial(lambda t, n: step(t, n), n=n) for n in range(count)]

    steps = [
        send_heads, lambda t: send_proj(t, (2,)), lambda t: send_proj(t, (1, 3)), relay_heads, project, *each(hide, 2),
        spread_own, *each(spread_partner, 2), relay_partner, *each(encode, PIECES), *each(sum_core, PIECES),
        *each(sum_near, PIECES), *each(activate, PIECES), *each(gather_far, PIECES), *each(gather_core, PIECES),
        decode, *each(sum_relay, 2), *each(sum_ring, 2), finish,
    ]
    for step, t in ORDER:
        steps[step](t)
    fetched("out")
    for t in range(chunks):
        settle(sent, send_sem, t)


def hand_on(features, rebuilt, features_out, rebuilt_out, first, second, came_in, went_out):
    parts = [(features, first, features_out)]
    parts += [(rebuilt.at[rows], second.at[rows], rebuilt_out.at[rows]) for rows in (pl.ds(0, 4), pl.ds(4, 4))]
    moves_in = [pltpu.make_async_copy(a, b, came_in.at[i]) for i, (a, b, _) in enumerate(parts)]
    moves_out = [pltpu.make_async_copy(b, c, went_out.at[i]) for i, (_, b, c) in enumerate(parts)]
    for move in moves_in:
        move.start()
    for move_in, move_out in zip(moves_in, moves_out):
        move_in.wait()
        move_out.start()
    for move in moves_out:
        move.wait()


def per_device(attn_heads, out_proj, resid_pre, enc_weight, enc_bias, dec_weight, dec_bias):
    _, tokens, slot = attn_heads.shape
    width = resid_pre.shape[2]
    feats = enc_weight.shape[2]
    per_owner = tokens // LAYERS
    chunks = per_owner // ROWS
    side = LAYERS * ROWS // 2
    two = 2 * slot
    vmem, anywhere = pl.BlockSpec(memory_space=pltpu.VMEM), pl.BlockSpec(memory_space=pl.ANY)
    shapes = (
        jax.ShapeDtypeStruct((per_owner, feats), F32),
        jax.ShapeDtypeStruct((8, 2, per_owner, slot), F32),
    )
    results = pl.pallas_call(
        functools.partial(kernel, chunks),
        out_shape=shapes,
        in_specs=[anywhere, anywhere, anywhere, anywhere, vmem, anywhere, vmem],
        out_specs=(anywhere, anywhere),
        scratch_shapes=[
            pltpu.VMEM((chunks, 2, 8, ROWS, 4 * slot), BF16),
            pltpu.VMEM((4 * slot, two), BF16),
            pltpu.VMEM((chunks, 2, 8, ROWS, slot), BF16),
            pltpu.VMEM((2, side, slot), BF16),
            pltpu.VMEM((2, side, slot), BF16),
            pltpu.VMEM((chunks - 1, 2, side, slot), F32),
            pltpu.VMEM((chunks - 1, 2, side, slot), F32),
            pltpu.VMEM((chunks, 2, side, slot), F32),
            pltpu.VMEM((chunks, 2 * side, width), BF16),
            pltpu.VMEM((width, feats), BF16),
            pltpu.VMEM((feats, width), BF16),
            pltpu.VMEM((chunks, 2 * side, feats), F32),
            pltpu.VMEM((chunks, side, feats), F32),
            pltpu.VMEM((chunks, 3, 2 * ROWS, feats), BF16),
            pltpu.VMEM((chunks, 3, 2 * ROWS, feats), BF16),
            pltpu.VMEM((chunks, 2 * ROWS, feats), F32),
            pltpu.VMEM((chunks, 2 * ROWS, feats), F32),
            pltpu.VMEM((chunks, 2 * side, feats), BF16),
            pltpu.VMEM((chunks, 2 * side, width), F32),
            pltpu.VMEM((chunks, 2, 2, side, slot), BF16),
            pltpu.VMEM((chunks, 2, 2, side, slot), BF16),
            pltpu.VMEM((chunks, 2, 2, 2, side, slot), BF16),
            pltpu.VMEM((chunks, 2, 2, 2, side, slot), BF16),
            pltpu.VMEM((chunks - 1, 2, side, slot), F32),
            pltpu.VMEM((chunks - 1, 2, side, slot), F32),
            pltpu.VMEM((2, side, slot), BF16),
            pltpu.VMEM((2, side, slot), BF16),
            pltpu.VMEM((chunks, 2 * ROWS, feats), F32),
            pltpu.VMEM((chunks, 2, 8, ROWS, slot), F32),
            pltpu.SemaphoreType.DMA((chunks,)),
            pltpu.SemaphoreType.DMA((ARRIVALS,)),
            pltpu.SemaphoreType.DMA((FETCHES,)),
        ],
        compiler_params=pltpu.CompilerParams(
            collective_id=0, has_side_effects=True, vmem_limit_bytes=66_000_000
        ),
        name="crosscoder",
    )(
        attn_heads.reshape(8, 2, per_owner, slot),
        out_proj[0],
        resid_pre.reshape(8, 2, per_owner, width),
        enc_weight[0],
        enc_bias.reshape(1, feats),
        dec_weight[0],
        dec_bias,
    )
    features, rebuilt = pl.pallas_call(
        hand_on,
        out_shape=shapes,
        in_specs=[anywhere, anywhere],
        out_specs=(anywhere, anywhere),
        scratch_shapes=[
            *(pltpu.VMEM(shape.shape, shape.dtype) for shape in shapes),
            pltpu.SemaphoreType.DMA((3,)),
            pltpu.SemaphoreType.DMA((3,)),
        ],
        name="hand_on",
    )(*results)
    return features, rebuilt.reshape(1, tokens, slot)


def solution(mesh):
    return jax.shard_map(
        per_device,
        mesh=mesh,
        in_specs=(
            P("layer", None, "feat"),
            P("layer", "feat", None),
            P("layer", None, None),
            P("layer", None, "feat"),
            P("feat"),
            P("layer", "feat", None),
            P("layer", "feat"),
        ),
        out_specs=(P("layer", "feat"), P("layer", None, "feat")),
        check_vma=False,
    )
```
